512 devices in a mesh: doc: 32 (over z_hi, y, core), lab: 16 (over z_lo, x).
Axes of the slice: x: 4, y: 8, z: 8 (z_hi: 2, z_lo: 4; z = z_hi * 4 + z_lo), core: 2. Of those that a mesh axis runs over, the one named last changes fastest.
Arguments:
- embeddings: bfloat16 [262144, 768], P(('doc', 'lab')), may hold values from -6 to 6
- positives: int32 [262144, 16], P(('doc', 'lab')), may hold values from 0 to 16383, as said below
- weights: float32 [131072, 768], P(('doc', 'lab')), may hold values from -6 to 6
- parents: int32 [131072], replicated, may hold values from 0 to 254, as said below
- owners: int32 [4, 32], replicated, may hold values from 0 to 15
- shortlist: int32 [4, 512, 4], replicated, may hold values from 0 to 3, as said below
- counts: int32 [4, 512], replicated, may hold values from 1 to 4, as said below
Outputs:
- trained: float32 [131072, 768], P(('doc', 'lab'))
- momentum: float32 [131072, 768], P(('doc', 'lab'))
The draws below stay inside these ranges and needn't reach their ends.
Inputs may be any that keep to these rules, and one draw needn't show every extreme that they name: `positives`: each positive code is (s * 16 + j) * 256 + l with s < 4, j < 16, l < 256; repeats allowed. parents[l] is a row of l's own block below l's row; row 0 of a block is its own parent. `shortlist`: the 4 tile numbers of one step and block are distinct. `counts`: in every step some block has all 4 slots live.
All inputs are finite; a program needn't handle non-finite values.
Results may differ from the reference program's by a relative error of at most 0.0003.
Values may be sent and summed in bfloat16 or wider, within the bound.
A program may use at most 64 MiB of HBM per device.

```python
import jax
import jax.numpy as jnp
from jax import lax

D = 768
BLOCK = 256
TILE = 128
PANEL = 512
MAXT = 4
POS = 16
STEPS = 4
DGROUPS = 32
LGROUPS = 16
TILES = 4
LBLOCKS = 512
LABELS = 131072
DOCS = 262144
N_LAB = 16


def draw_positives(key, part):
    rows = DGROUPS * LGROUPS * PANEL
    key_step, key_lab, key_off = jax.random.split(jax.random.fold_in(key, 11), 3)
    step = jax.random.randint(key_step, (rows, POS), 0, STEPS)
    label_group = jax.random.randint(key_lab, (rows, POS), 0, LGROUPS)
    offset = jax.random.randint(key_off, (rows, POS), 0, BLOCK)
    result = ((step * LGROUPS + label_group) * BLOCK + offset).astype(jnp.int32)
    result = result.at[0, 0].set(0)
    result = result.at[rows - 1, POS - 1].set(STEPS * LGROUPS * BLOCK - 1)
    return result


def draw_parents(key, part):
    local = jnp.arange(LABELS, dtype=jnp.int32) % BLOCK
    picked = jax.random.randint(jax.random.fold_in(key, 12), (LABELS,), 0, jnp.maximum(local, 1))
    picked = jnp.where(local == 0, 0, picked)
    picked = jnp.where(local == BLOCK - 1, BLOCK - 2, picked)
    return picked.astype(jnp.int32)


def draw_shortlist(key, part):
    keys = jax.random.split(jax.random.fold_in(key, 13), STEPS * LBLOCKS)
    picks = jax.vmap(lambda one_key: jax.random.permutation(one_key, TILES)[:MAXT])(keys)
    return picks.reshape(STEPS, LBLOCKS, MAXT).astype(jnp.int32)


def draw_counts(key, part):
    key_level, key_full = jax.random.split(jax.random.fold_in(key, 14))
    result = jax.random.randint(key_level, (STEPS, LBLOCKS), 1, MAXT + 1)
    full_block = jax.random.randint(key_full, (STEPS,), 0, LBLOCKS)
    result = result.at[jnp.arange(STEPS), full_block].set(MAXT)
    return result.astype(jnp.int32)


def plant(drawn, rng, least, largest):
    extent = drawn.shape
    place = [jax.random.randint(jax.random.fold_in(rng, axis), (), 0, extent[axis]) for axis in range(len(extent))]
    drawn = drawn.at[tuple(place)].set(least)
    longest = extent.index(max(extent))
    place[longest] = (place[longest] + 1) % extent[longest]
    return drawn.at[tuple(place)].set(largest)


def shard_levels(own_key, shape, cuts, smallest, largest):
    level = 1.0
    for position, blocks in cuts:
        steps = jax.random.uniform(jax.random.fold_in(jax.random.fold_in(own_key, 6), position), (blocks,), jnp.float32, smallest / len(cuts), largest / len(cuts))
        level = level * jnp.repeat(jnp.exp(steps), shape[position] // blocks).reshape((-1,) + (1,) * (len(shape) - 1 - position))
    return level


def gaussian(own_key, shape, spread, bound, cuts=(), kind=jnp.bfloat16):
    array = jax.random.normal(own_key, shape, jnp.float32) * spread
    if len(cuts) > 0:
        array = shard_levels(own_key, shape, cuts, -0.22, 0.18) * array
    return jnp.clip(array, min=-bound, max=bound).astype(kind)


def setup_inputs(seed: int = 0) -> dict:
    seeds = jax.random.split(jax.random.key(seed), 8)
    embeddings = gaussian(seeds[0], (DOCS, D), 1.0, 6.0, ((0, 512),))
    positives = draw_positives(jax.random.fold_in(seeds[7], 71), 0)
    weights = gaussian(seeds[2], (LABELS, D), 1.0, 6.0, ((0, 512),), jnp.float32)
    parents = draw_parents(jax.random.fold_in(seeds[7], 71), 0)
    owners = plant(jax.random.randint(seeds[4], (STEPS, DGROUPS), 0, N_LAB), jax.random.fold_in(seeds[4], 1), 0, N_LAB - 1).astype(jnp.int32)
    shortlist = draw_shortlist(jax.random.fold_in(seeds[7], 71), 0)
    counts = draw_counts(jax.random.fold_in(seeds[7], 71), 0)
    return {"embeddings": embeddings, "positives": positives, "weights": weights, "parents": parents, "owners": owners, "shortlist": shortlist, "counts": counts}


learning_rate = 0.1
beta_rate = 0.9
pull_rate = 1.0

def pick_rows(panel, labels, tiles, tile_rows):
    width = panel.shape[1]
    shaped = panel.reshape(panel.shape[0] // tile_rows, tile_rows, width)
    lshaped = labels.reshape(labels.shape[0] // tile_rows, tile_rows, labels.shape[1])
    rows = jnp.take(shaped, tiles, axis=0).reshape(tiles.shape[0] * tile_rows, width)
    picked = jnp.take(lshaped, tiles, axis=0).reshape(tiles.shape[0] * tile_rows, labels.shape[1])
    return (rows, picked)

def block_update(weight, moment, rows, picked, base, parent_rows, live):
    scale = 1.0 / jnp.sqrt(jnp.float32(rows.shape[1]))
    rows32 = rows.astype(jnp.float32)
    scores = jnp.dot(rows32, weight.T, precision=lax.Precision.HIGHEST, preferred_element_type=jnp.float32) * scale
    label_ids = base + jnp.arange(weight.shape[0], dtype=jnp.int32)
    target = jnp.any(picked[:, :, None] == label_ids[None, None, :], axis=1).astype(jnp.float32)
    resid = (jax.nn.sigmoid(scores) - target) * live[:, None]
    grad = jnp.dot(resid.T, rows32, precision=lax.Precision.HIGHEST, preferred_element_type=jnp.float32) * scale
    grad = grad + pull_rate * (weight - jnp.take(weight, parent_rows, axis=0))
    moment = beta_rate * moment + grad
    return (weight - learning_rate * moment, moment)

def reference(embeddings, positives, weights, parents, owners, shortlist, counts):
    blocks = weights.reshape(LBLOCKS, BLOCK, D)
    moments = jnp.zeros((LBLOCKS, BLOCK, D), jnp.float32)
    parent_blocks = parents.reshape(LBLOCKS, BLOCK)
    slot_of_row = jnp.arange(MAXT * TILE, dtype=jnp.int32) // TILE
    for step in range(STEPS):

        def one(item):
            index, weight, moment, parent_rows = item
            anchor = index // LGROUPS
            holder = (anchor + step) % DGROUPS
            owner = owners[step, holder]
            start = ((holder * LGROUPS + owner) * PANEL).astype(jnp.int32)
            panel = lax.dynamic_slice_in_dim(embeddings, start, PANEL, 0)
            labels = lax.dynamic_slice_in_dim(positives, start, PANEL, 0)
            rows, picked = pick_rows(panel, labels, shortlist[step, index], TILE)
            live = (slot_of_row < counts[step, index]).astype(jnp.float32)
            base = ((step * LGROUPS + index % LGROUPS) * BLOCK).astype(jnp.int32)
            return block_update(weight, moment, rows, picked, base, parent_rows, live)
        blocks, moments = lax.map(one, (jnp.arange(LBLOCKS, dtype=jnp.int32), blocks, moments, parent_blocks))
    return (blocks.reshape(LABELS, D), moments.reshape(LABELS, D))
```

```python
import functools

import jax
import jax.numpy as jnp
from jax import lax
from jax.experimental import pallas as pl
from jax.experimental.pallas import tpu as pltpu
from jax.sharding import PartitionSpec as P

MESH = pl.DeviceIdType.MESH

TILE = 128
STEPS = 4
RING = 4

learning_rate = 0.1
beta_rate = 0.9
pull_rate = 1.0


def split(value):
    high = value.astype(jnp.bfloat16)
    low = (value - high.astype(jnp.float32)).astype(jnp.bfloat16)
    return high, low


def train_kernel(
    doc_count,
    owners,
    counts,
    shortlist,
    parents,
    embeddings,
    positives,
    weights,
    trained,
    momentum,
    emb,
    pos,
    par,
    pull,
    src,
    row,
    shift,
    cand,
    inward,
    outward,
    arrived,
    panel,
    load_sem,
    row_send,
    row_recv,
    shift_send,
    shift_recv,
    in_send,
    out_send,
    line_recv,
    ring_send,
    ring_recv,
    pass_send,
    pass_recv,
):
    doc = lax.axis_index("doc")
    lab = lax.axis_index("lab")
    z, x = lab // RING, lab % RING
    block = doc * (RING * RING) + lab
    width = embeddings.shape[1]
    lanes = width // TILE
    code_rows = lanes * TILE
    tile_rows = src.shape[1]
    half = tile_rows // 2
    picks = positives.shape[0]
    labels = weights.shape[0]
    scale = 1.0 / (float(width) ** 0.5)

    def at_x(k):
        return (doc, z * RING + (x + k) % RING)

    def at_z(to):
        return (doc, to * RING + x)

    def at_doc(k):
        return ((doc + k) % doc_count, lab)

    low_half = z < RING // 2
    side = jnp.where(low_half, 0, 1)
    far = jnp.where(low_half, z + 1, z - 1)
    near = jnp.where(low_half, z - 1, z + 1)
    has_near = (z % (RING - 1)) != 0

    loads = [
        pltpu.make_async_copy(embeddings, emb, load_sem.at[0]),
        pltpu.make_async_copy(positives, pos, load_sem.at[1]),
        pltpu.make_async_copy(weights, trained, load_sem.at[2]),
        pltpu.make_async_copy(parents.at[pl.ds(8 * (block // 4), 8)], par, load_sem.at[3]),
    ]
    for load in loads:
        load.start()

    barrier = pltpu.get_barrier_semaphore()
    partners = [at_x(k) for k in range(1, RING)]
    for k in range(1, STEPS):
        partners += [at_doc(k), at_doc(-k)]
    partners.append(at_z(far))
    for partner in partners:
        pl.semaphore_signal(barrier, inc=1, device_id=partner, device_id_type=MESH)

    @pl.when(has_near)
    def _():
        pl.semaphore_signal(barrier, inc=1, device_id=at_z(near), device_id_type=MESH)

    loads[0].wait()
    loads[1].wait()
    for t in range(RING):
        for c in range(lanes):
            src[t, pl.ds(c * TILE, TILE), :] = emb[pl.ds(t * TILE, TILE), pl.ds(c * TILE, TILE)]
        code = pos[:, pl.ds(t * TILE, TILE)]
        src[t, pl.ds(code_rows, picks), :] = (code // labels).astype(jnp.float32).astype(jnp.bfloat16)
        src[t, pl.ds(code_rows + picks, picks), :] = (code % labels).astype(jnp.float32).astype(jnp.bfloat16)
    row[x] = src[x]

    pl.semaphore_wait(barrier, len(partners) + jnp.where(has_near, 1, 0))

    def remote(source, target, send, recv, device):
        return pltpu.make_async_remote_copy(
            src_ref=source,
            dst_ref=target,
            send_sem=send,
            recv_sem=recv,
            device_id=device,
            device_id_type=MESH,
        )

    row_copies = []
    for k in range(1, RING):
        to = (x + k) % RING
        row_copies.append(
            remote(src.at[to], row.at[x], row_send.at[k - 1], row_recv.at[k - 1], at_x(k))
        )
    for copy in row_copies:
        copy.start()

    loads[3].wait()
    ids = lax.broadcasted_iota(jnp.int32, (labels, TILE), 0)
    columns = []
    for c in range(labels // TILE):
        parent = par[pl.ds((block % 4) * (labels // TILE) + c, 1), :]
        own = lax.broadcasted_iota(jnp.int32, (labels, TILE), 1) + c * TILE
        columns.append(
            (ids == own).astype(jnp.float32) - (ids == parent).astype(jnp.float32)
        )
    pull[...] = jnp.transpose(jnp.concatenate(columns, axis=1)).astype(jnp.bfloat16)
    momentum[...] = jnp.zeros_like(momentum)
    loads[2].wait()

    for copy in row_copies:
        copy.wait_recv()

    shift_copies = {}
    for s in range(1, STEPS):
        shift_copies[s] = remote(
            shift.at[s - 1],
            cand.at[s],
            shift_send.at[s - 1],
            shift_recv.at[s - 1],
            at_doc(-s),
        )

    def choose(s):
        picked = row[owners[s, doc] % RING]
        if s == 0:
            cand[0] = picked
        else:
            shift[s - 1] = picked
            shift_copies[s].start()

    def owner_z(s):
        return owners[s, (doc + s) % doc_count] // RING

    def line_in(s):
        return remote(
            inward.at[s], arrived.at[side, s], in_send.at[s], line_recv.at[side, s], at_z(far)
        )

    def line_out(s):
        return remote(
            outward.at[s],
            arrived.at[1 - side, s],
            out_send.at[s],
            line_recv.at[1 - side, s],
            at_z(near),
        )

    def wait_near(s):
        remote(
            inward.at[s], arrived.at[side, s], in_send.at[s], line_recv.at[side, s], at_z(far)
        ).wait_recv()

    def wait_far(s):
        remote(
            outward.at[s], arrived.at[1 - side, s], out_send.at[s], line_recv.at[1 - side, s], at_z(far)
        ).wait_recv()

    def flow_in(s):
        if s > 0:
            shift_copies[s].wait_recv()

        @pl.when(has_near)
        def _():
            wait_near(s)
            inward[s] = jnp.where(owner_z(s) == z, cand[s], arrived[side, s])

        @pl.when(jnp.logical_not(has_near))
        def _():
            inward[s] = cand[s]

        line_in(s).start()

    def ring_copies(s):
        return (
            remote(panel.at[s, x], panel.at[s, x], ring_send.at[0, s], ring_recv.at[0, s], at_x(1)),
            remote(panel.at[s, x], panel.at[s, x], ring_send.at[1, s], ring_recv.at[1, s], at_x(-1)),
        )

    def pass_copies(s):
        left = (x + RING - 1) % RING
        right = (x + 1) % RING
        first = panel.at[s, left, pl.ds(0, half)]
        second = panel.at[s, right, pl.ds(half, half)]
        return (
            remote(first, first, pass_send.at[0, s], pass_recv.at[0, s], at_x(1)),
            remote(second, second, pass_send.at[1, s], pass_recv.at[1, s], at_x(-1)),
        )

    def flow_out(s):
        wait_far(s)
        mine = owner_z(s) == z

        @pl.when(has_near)
        def _():
            outward[s] = jnp.where(mine, cand[s], arrived[1 - side, s])
            line_out(s).start()
            nearer = jnp.where(low_half, owner_z(s) <= z, owner_z(s) >= z)
            panel[s, x] = jnp.where(nearer, inward[s], arrived[1 - side, s])

        @pl.when(jnp.logical_not(has_near))
        def _():
            panel[s, x] = jnp.where(mine, cand[s], arrived[1 - side, s])

        for copy in ring_copies(s):
            copy.start()

    def ring_pass(s):
        for copy in ring_copies(s):
            copy.wait_recv()
        for copy in pass_copies(s):
            copy.start()

    def tile_rows_of(s, t):
        return jnp.concatenate(
            [panel[s, t, pl.ds(c * TILE, TILE), :] for c in range(lanes)], axis=1
        )

    def update(s):
        for copy in pass_copies(s):
            copy.wait_recv()
        high, low = split(trained[...])
        count = counts[s, block]
        grad = None
        for pair in range(RING // 2):
            tiles = (2 * pair, 2 * pair + 1)
            rows = jnp.concatenate([tile_rows_of(s, t) for t in tiles], axis=0)
            contract = (((1,), (1,)), ((), ()))
            scores = (
                lax.dot_general(high, rows, contract, preferred_element_type=jnp.float32)
                + lax.dot_general(low, rows, contract, preferred_element_type=jnp.float32)
            ) * scale
            keys, lives = [], []
            for t in tiles:
                group = panel[s, t, pl.ds(code_rows, picks), :].astype(jnp.float32)
                label = panel[s, t, pl.ds(code_rows + picks, picks), :].astype(jnp.float32)
                wanted = (s * RING * RING + lab).astype(jnp.float32)
                keys.append(jnp.where(group == wanted, label, -1.0))
                live = jnp.float32(0.0)
                for k in range(RING):
                    met = jnp.logical_and(count > k, shortlist[s, k, block] == t)
                    live = jnp.where(met, jnp.float32(1.0), live)
                lives.append(jnp.full((1, TILE), live, jnp.float32))
            keys = jnp.concatenate(keys, axis=1)
            lives = jnp.concatenate(lives, axis=1)
            names = lax.broadcasted_iota(jnp.int32, scores.shape, 0).astype(jnp.float32)
            hit = names == keys[0:1, :]
            for p in range(1, picks):
                hit = jnp.logical_or(hit, names == keys[p : p + 1, :])
            resid = (jax.nn.sigmoid(scores) - jnp.where(hit, 1.0, 0.0)) * lives
            rhigh, rlow = split(resid)
            part = jnp.dot(rhigh, rows, preferred_element_type=jnp.float32) + jnp.dot(
                rlow, rows, preferred_element_type=jnp.float32
            )
            grad = part if grad is None else grad + part
        pulled = jnp.dot(pull[...], high, preferred_element_type=jnp.float32) + jnp.dot(
            pull[...], low, preferred_element_type=jnp.float32
        )
        moment = beta_rate * momentum[...] + (grad * scale + pull_rate * pulled)
        momentum[...] = moment
        trained[...] = trained[...] - learning_rate * moment

    choose(0)
    flow_in(0)
    for s in range(1, STEPS):
        choose(s)
    flow_in(1)
    flow_out(0)
    flow_in(2)
    flow_out(1)
    ring_pass(0)
    flow_in(3)
    flow_out(2)
    ring_pass(1)
    update(0)
    flow_out(3)
    ring_pass(2)
    update(1)
    ring_pass(3)
    update(2)
    update(3)

    for copy in row_copies:
        copy.wait_send()
    for s in range(1, STEPS):
        shift_copies[s].wait_send()
    for s in range(STEPS):
        line_in(s).wait_send()

        @pl.when(has_near)
        def _():
            line_out(s).wait_send()

        for copy in ring_copies(s) + pass_copies(s):
            copy.wait_send()


def local(doc_count, embeddings, positives, weights, parents, owners, shortlist, counts):
    rows, width = embeddings.shape
    labels = weights.shape[0]
    picks = positives.shape[1]
    tile_rows = width + 2 * picks
    tile = (tile_rows, TILE)
    half = jnp.bfloat16
    dma = pltpu.SemaphoreType.DMA
    out = jax.ShapeDtypeStruct(weights.shape, jnp.float32)
    smem = pl.BlockSpec(memory_space=pltpu.SMEM)
    hbm = pl.BlockSpec(memory_space=pl.ANY)
    vmem = pl.BlockSpec(memory_space=pltpu.VMEM)
    return pl.pallas_call(
        functools.partial(train_kernel, doc_count),
        out_shape=(out, out),
        in_specs=[smem, smem, smem, hbm, hbm, hbm, hbm],
        out_specs=(vmem, vmem),
        scratch_shapes=[
            pltpu.VMEM((rows, width), half),
            pltpu.VMEM((picks, rows), jnp.int32),
            pltpu.VMEM((8, TILE), jnp.int32),
            pltpu.VMEM((labels, labels), half),
            pltpu.VMEM((RING,) + tile, half),
            pltpu.VMEM((RING,) + tile, half),
            pltpu.VMEM((STEPS - 1,) + tile, half),
            pltpu.VMEM((STEPS,) + tile, half),
            pltpu.VMEM((STEPS,) + tile, half),
            pltpu.VMEM((STEPS,) + tile, half),
            pltpu.VMEM((2, STEPS) + tile, half),
            pltpu.VMEM((STEPS, RING) + tile, half),
            dma((4,)),
            dma((RING - 1,)),
            dma((RING - 1,)),
            dma((STEPS - 1,)),
            dma((STEPS - 1,)),
            dma((STEPS,)),
            dma((STEPS,)),
            dma((2, STEPS)),
            dma((2, STEPS)),
            dma((2, STEPS)),
            dma((2, STEPS)),
            dma((2, STEPS)),
        ],
        compiler_params=pltpu.CompilerParams(
            collective_id=0, has_side_effects=True, vmem_limit_bytes=48 * 1024 * 1024
        ),
    )(
        owners,
        counts,
        jnp.transpose(shortlist, (0, 2, 1)),
        parents.reshape(-1, TILE),
        embeddings,
        positives.T,
        weights,
    )


def solution(mesh):
    return jax.shard_map(
        functools.partial(local, mesh.shape["doc"]),
        mesh=mesh,
        in_specs=(
            P(("doc", "lab"), None),
            P(("doc", "lab"), None),
            P(("doc", "lab"), None),
            P(),
            P(),
            P(),
            P(),
        ),
        out_specs=(P(("doc", "lab"), None), P(("doc", "lab"), None)),
        check_vma=False,
    )
```

```python
import functools

import jax
import jax.numpy as jnp
from jax import lax
from jax.experimental import pallas as pl
from jax.experimental.pallas import tpu as pltpu
from jax.sharding import PartitionSpec as P

MESH = pl.DeviceIdType.MESH

TILE = 128
STEPS = 4
RING = 4
PARTS = 2

learning_rate = 0.1
beta_rate = 0.9
pull_rate = 1.0


def split(value):
    high = value.astype(jnp.bfloat16)
    low = (value - high.astype(jnp.float32)).astype(jnp.bfloat16)
    return high, low


def train_kernel(
    doc_count,
    owners_all,
    counts_all,
    shortlist_all,
    parents,
    embeddings,
    positives,
    weights,
    trained,
    momentum,
    owners,
    counts,
    shortlist,
    emb,
    pos,
    par,
    pull,
    src,
    row_first,
    row_second,
    cand,
    inward,
    outward,
    arrived,
    ready,
    panel,
    load_sem,
    row_send,
    row_recv,
    in_send,
    out_send,
    line_recv,
    shift_send,
    shift_recv,
    spread_send,
    ring_send,
    ring_recv,
    pass_send,
    pass_recv,
):
    doc = lax.axis_index("doc")
    lab = lax.axis_index("lab")
    z, x = lab // RING, lab % RING
    block = doc * (RING * RING) + lab
    width = embeddings.shape[1]
    lanes = width // TILE
    code_rows = lanes * TILE
    part_rows = src.shape[1] // PARTS
    picks = positives.shape[0]
    labels = weights.shape[0]
    scale = 1.0 / (float(width) ** 0.5)
    row = (row_first, row_second)
    span = doc_count // 2
    place = doc % span

    def at_x(k):
        return (doc, z * RING + (x + k) % RING)

    def at_z(to):
        return (doc, to * RING + x)

    def across(k, crosses):
        to_z = jnp.where(crosses, RING - 1 - z, z)
        return ((doc + k) % doc_count, to_z * RING + x)

    sends_over = [place < s for s in range(STEPS)]
    takes_over = [place + s >= span for s in range(STEPS)]

    low_half = z < RING // 2
    side = jnp.where(low_half, 0, 1)
    far = jnp.where(low_half, z + 1, z - 1)
    near = jnp.where(low_half, z - 1, z + 1)
    has_near = (z % (RING - 1)) != 0

    lane_block = pl.ds(TILE * (block // TILE), TILE)
    loads = [
        pltpu.make_async_copy(embeddings, emb, load_sem.at[0]),
        pltpu.make_async_copy(positives, pos, load_sem.at[1]),
        pltpu.make_async_copy(owners_all, owners, load_sem.at[2]),
        pltpu.make_async_copy(counts_all.at[:, lane_block], counts, load_sem.at[3]),
        pltpu.make_async_copy(shortlist_all.at[:, :, lane_block], shortlist, load_sem.at[4]),
        pltpu.make_async_copy(parents.at[pl.ds(8 * (block // 4), 8)], par, load_sem.at[5]),
        pltpu.make_async_copy(weights, trained, load_sem.at[6]),
    ]
    for load in loads:
        load.start()

    barrier = pltpu.get_barrier_semaphore()
    partners = [at_x(k) for k in range(1, RING)]
    for s in range(1, STEPS):
        partners += [across(-s, sends_over[s]), across(s, takes_over[s])]
    partners.append(at_z(far))
    for partner in partners:
        pl.semaphore_signal(barrier, inc=1, device_id=partner, device_id_type=MESH)

    @pl.when(has_near)
    def _():
        pl.semaphore_signal(barrier, inc=1, device_id=at_z(near), device_id_type=MESH)

    loads[0].wait()
    loads[1].wait()
    for t in range(RING):
        for c in range(lanes):
            src[t, pl.ds(c * TILE, TILE), :] = emb[pl.ds(t * TILE, TILE), pl.ds(c * TILE, TILE)]
        code = pos[:, pl.ds(t * TILE, TILE)]
        src[t, pl.ds(code_rows, picks), :] = (code // labels).astype(jnp.float32).astype(jnp.bfloat16)
        src[t, pl.ds(code_rows + picks, picks), :] = (code % labels).astype(jnp.float32).astype(jnp.bfloat16)
    for h in range(PARTS):
        row[h][x] = src[x, pl.ds(h * part_rows, part_rows), :]

    pl.semaphore_wait(barrier, len(partners) + jnp.where(has_near, 1, 0))

    def remote(source, target, send, recv, device):
        return pltpu.make_async_remote_copy(
            src_ref=source,
            dst_ref=target,
            send_sem=send,
            recv_sem=recv,
            device_id=device,
            device_id_type=MESH,
        )

    parts = [pl.ds(h * part_rows, part_rows) for h in range(PARTS)]

    def row_copies(h):
        return [
            remote(
                src.at[(x + k) % RING, parts[h]],
                row[h].at[x],
                row_send.at[h, k - 1],
                row_recv.at[h, k - 1],
                at_x(k),
            )
            for k in range(1, RING)
        ]

    def row_start(h):
        for copy in row_copies(h):
            copy.start()

    def row_wait(h):
        for copy in row_copies(h):
            copy.wait_recv()

    def owner_z(s, home):
        return owners[s, home] // RING

    def line_in(h, s):
        return remote(
            inward.at[s, parts[h]],
            arrived.at[side, s, parts[h]],
            in_send.at[h, s],
            line_recv.at[side, h, s],
            at_z(far),
        )

    def line_out(h, s, to):
        return remote(
            outward.at[s, parts[h]],
            arrived.at[1 - side, s, parts[h]],
            out_send.at[h, s],
            line_recv.at[1 - side, h, s],
            at_z(to),
        )

    def goes_in(h, s):
        return jnp.logical_or(jnp.logical_not(sends_over[s]), side == h)

    def goes_out(h, s):
        return jnp.logical_or(jnp.logical_not(sends_over[s]), side != h)

    def over_copy(h, s):
        target = panel.at[s, x, parts[h]]
        return remote(
            outward.at[s, parts[h]], target, shift_send.at[h, s], shift_recv.at[h, s], across(-s, True)
        )

    def shift_copy(h, s):
        target = panel.at[s, x, parts[h]]
        return remote(
            ready.at[s, parts[h]], target, shift_send.at[h, s], shift_recv.at[h, s], across(-s, False)
        )

    def flow_in(h, s):
        cand[s, parts[h], :] = row[h][owners[s, doc] % RING]

        @pl.when(goes_in(h, s))
        def _():
            @pl.when(has_near)
            def _():
                line_in(h, s).wait_recv()
                inward[s, parts[h], :] = jnp.where(
                    owner_z(s, doc) == z, cand[s, parts[h], :], arrived[side, s, parts[h], :]
                )

            @pl.when(jnp.logical_not(has_near))
            def _():
                inward[s, parts[h], :] = cand[s, parts[h], :]

            line_in(h, s).start()

    def flow_out(h, s):
        mine = owner_z(s, doc) == z

        @pl.when(goes_out(h, s))
        def _():
            line_out(h, s, far).wait_recv()
            outward[s, parts[h], :] = jnp.where(
                mine, cand[s, parts[h], :], arrived[1 - side, s, parts[h], :]
            )

            @pl.when(has_near)
            def _():
                line_out(h, s, near).start()

        over = jnp.logical_and(sends_over[s], side != h)

        @pl.when(jnp.logical_and(over, jnp.logical_not(has_near)))
        def _():
            over_copy(h, s).start()

        @pl.when(jnp.logical_not(sends_over[s]))
        def _():
            nearer = jnp.where(low_half, owner_z(s, doc) <= z, owner_z(s, doc) >= z)
            merged = jnp.where(nearer, inward[s, parts[h], :], arrived[1 - side, s, parts[h], :])
            if s == 0:
                panel[s, x, parts[h], :] = merged
            else:
                ready[s, parts[h], :] = merged
                shift_copy(h, s).start()

    def spread_copy(h, s):
        part = panel.at[s, x, parts[h]]
        to = z + 1 if h < PARTS // 2 else z - 1
        return remote(part, part, spread_send.at[h, s], shift_recv.at[h, s], at_z(to))

    def spreads(h, s):
        more = z < RING - 1 if h < PARTS // 2 else z > 0
        return jnp.logical_and(takes_over[s], more)

    def ring_copies(h, s):
        part = panel.at[s, x, parts[h]]
        return (
            remote(part, part, ring_send.at[0, h, s], ring_recv.at[0, h, s], at_x(1)),
            remote(part, part, ring_send.at[1, h, s], ring_recv.at[1, h, s], at_x(-1)),
        )

    def gather(h, s):
        if s > 0:
            shift_copy(h, s).wait_recv()

            @pl.when(spreads(h, s))
            def _():
                spread_copy(h, s).start()

        for copy in ring_copies(h, s):
            copy.start()

    def pass_copy(h, s):
        forth = 1 if h < PARTS // 2 else -1
        part = panel.at[s, (x + RING - forth) % RING, parts[h]]
        return remote(part, part, pass_send.at[h, s], pass_recv.at[h, s], at_x(forth))

    def ring_pass(h, s):
        for copy in ring_copies(h, s):
            copy.wait_recv()
        pass_copy(h, s).start()

    def tile_rows_of(s, t):
        return jnp.concatenate(
            [panel[s, t, pl.ds(c * TILE, TILE), :] for c in range(lanes)], axis=1
        )

    def update(s):
        for h in range(PARTS):
            pass_copy(h, s).wait_recv()
        high, low = split(trained[...])
        count = counts[s, block % TILE]
        grad = None
        for pair in range(RING // 2):
            tiles = (2 * pair, 2 * pair + 1)
            rows = jnp.concatenate([tile_rows_of(s, t) for t in tiles], axis=0)
            contract = (((1,), (1,)), ((), ()))
            scores = (
                lax.dot_general(high, rows, contract, preferred_element_type=jnp.float32)
                + lax.dot_general(low, rows, contract, preferred_element_type=jnp.float32)
            ) * scale
            keys, lives = [], []
            for t in tiles:
                group = panel[s, t, pl.ds(code_rows, picks), :].astype(jnp.float32)
                label = panel[s, t, pl.ds(code_rows + picks, picks), :].astype(jnp.float32)
                wanted = (s * RING * RING + lab).astype(jnp.float32)
                keys.append(jnp.where(group == wanted, label, -1.0))
                live = jnp.float32(0.0)
                for k in range(RING):
                    met = jnp.logical_and(count > k, shortlist[s, k, block % TILE] == t)
                    live = jnp.where(met, jnp.float32(1.0), live)
                lives.append(jnp.full((1, TILE), live, jnp.float32))
            keys = jnp.concatenate(keys, axis=1)
            lives = jnp.concatenate(lives, axis=1)
            names = lax.broadcasted_iota(jnp.int32, scores.shape, 0).astype(jnp.float32)
            hit = names == keys[0:1, :]
            for p in range(1, picks):
                hit = jnp.logical_or(hit, names == keys[p : p + 1, :])
            resid = (jax.nn.sigmoid(scores) - jnp.where(hit, 1.0, 0.0)) * lives
            rhigh, rlow = split(resid)
            part = jnp.dot(rhigh, rows, preferred_element_type=jnp.float32) + jnp.dot(
                rlow, rows, preferred_element_type=jnp.float32
            )
            grad = part if grad is None else grad + part
        pulled = jnp.dot(pull[...], high, preferred_element_type=jnp.float32) + jnp.dot(
            pull[...], low, preferred_element_type=jnp.float32
        )
        moment = beta_rate * momentum[...] + (grad * scale + pull_rate * pulled)
        momentum[...] = moment
        trained[...] = trained[...] - learning_rate * moment

    row_start(0)

    loads[5].wait()
    ids = lax.broadcasted_iota(jnp.int32, (labels, TILE), 0)
    columns = []
    for c in range(labels // TILE):
        parent = par[pl.ds((block % 4) * (labels // TILE) + c, 1), :]
        own = lax.broadcasted_iota(jnp.int32, (labels, TILE), 1) + c * TILE
        columns.append((ids == own).astype(jnp.float32) - (ids == parent).astype(jnp.float32))
    pull[...] = jnp.transpose(jnp.concatenate(columns, axis=1)).astype(jnp.bfloat16)
    momentum[...] = jnp.zeros_like(momentum)
    for load in (loads[2], loads[3], loads[4], loads[6]):
        load.wait()

    row_wait(0)
    row_start(1)
    for s in range(STEPS):
        flow_in(0, s)
    flow_out(0, 0)
    row_wait(1)
    order = [(h, s) for h in range(PARTS) for s in range(STEPS)]
    for i in range(1, len(order)):
        if i <= STEPS:
            flow_in(1, i - 1)
        flow_out(*order[i])
        gather(*order[i - 1])
        if i >= 2:
            ring_pass(*order[i - 2])
    update(0)
    gather(*order[-1])
    ring_pass(*order[-2])
    update(1)
    ring_pass(*order[-1])
    update(2)
    update(3)

    for h in range(PARTS):
        for copy in row_copies(h):
            copy.wait_send()
        for s in range(STEPS):

            @pl.when(goes_in(h, s))
            def _():
                line_in(h, s).wait_send()

            @pl.when(jnp.logical_and(goes_out(h, s), has_near))
            def _():
                line_out(h, s, near).wait_send()

            if s > 0:
                ends = jnp.logical_and(side != h, jnp.logical_not(has_near))

                @pl.when(jnp.logical_or(jnp.logical_not(sends_over[s]), ends))
                def _():
                    shift_copy(h, s).wait_send()

                @pl.when(spreads(h, s))
                def _():
                    spread_copy(h, s).wait_send()

            for copy in ring_copies(h, s):
                copy.wait_send()
            pass_copy(h, s).wait_send()


def local(doc_count, embeddings, positives, weights, parents, owners, shortlist, counts):
    rows, width = embeddings.shape
    labels = weights.shape[0]
    picks = positives.shape[1]
    slots = shortlist.shape[2]
    tile = (width + 2 * picks, TILE)
    half = jnp.bfloat16
    dma = pltpu.SemaphoreType.DMA
    out = jax.ShapeDtypeStruct(weights.shape, jnp.float32)
    hbm = pl.BlockSpec(memory_space=pltpu.HBM)
    vmem = pl.BlockSpec(memory_space=pltpu.VMEM)
    return pl.pallas_call(
        functools.partial(train_kernel, doc_count),
        out_shape=(out, out),
        in_specs=[hbm] * 7,
        out_specs=(vmem, vmem),
        scratch_shapes=[
            pltpu.SMEM(owners.shape, jnp.int32),
            pltpu.SMEM((STEPS, TILE), jnp.int32),
            pltpu.SMEM((STEPS, slots, TILE), jnp.int32),
            pltpu.VMEM((rows, width), half),
            pltpu.VMEM((picks, rows), jnp.int32),
            pltpu.VMEM((8, TILE), jnp.int32),
            pltpu.VMEM((labels, labels), half),
            pltpu.VMEM((RING,) + tile, half),
            pltpu.VMEM((RING, tile[0] // PARTS, TILE), half),
            pltpu.VMEM((RING, tile[0] // PARTS, TILE), half),
            pltpu.VMEM((STEPS,) + tile, half),
            pltpu.VMEM((STEPS,) + tile, half),
            pltpu.VMEM((STEPS,) + tile, half),
            pltpu.VMEM((2, STEPS) + tile, half),
            pltpu.VMEM((STEPS,) + tile, half),
            pltpu.VMEM((STEPS, RING) + tile, half),
            dma((7,)),
            dma((PARTS, RING - 1)),
            dma((PARTS, RING - 1)),
            dma((PARTS, STEPS)),
            dma((PARTS, STEPS)),
            dma((2, PARTS, STEPS)),
            dma((PARTS, STEPS)),
            dma((PARTS, STEPS)),
            dma((PARTS, STEPS)),
            dma((2, PARTS, STEPS)),
            dma((2, PARTS, STEPS)),
            dma((PARTS, STEPS)),
            dma((PARTS, STEPS)),
        ],
        compiler_params=pltpu.CompilerParams(
            collective_id=0, has_side_effects=True, vmem_limit_bytes=48 * 1024 * 1024
        ),
    )(
        *(
            pltpu.with_memory_space_constraint(value, pltpu.HBM)
            for value in (
                owners,
                counts,
                jnp.transpose(shortlist, (0, 2, 1)),
                parents.reshape(-1, TILE),
                embeddings,
                positives.T,
                weights,
            )
        )
    )


def solution(mesh):
    return jax.shard_map(
        functools.partial(local, mesh.shape["doc"]),
        mesh=mesh,
        in_specs=(
            P(("doc", "lab"), None),
            P(("doc", "lab"), None),
            P(("doc", "lab"), None),
            P(),
            P(),
            P(),
            P(),
        ),
        out_specs=(P(("doc", "lab"), None), P(("doc", "lab"), None)),
        check_vma=False,
    )
```

```python
import functools

import jax
import jax.numpy as jnp
from jax import lax
from jax.experimental import pallas as pl
from jax.experimental.pallas import tpu as pltpu
from jax.sharding import PartitionSpec as P

MESH = pl.DeviceIdType.MESH

TILE = 128
STEPS = 4
RING = 4
PARTS = 2
OUT_LAG, GATHER_LAG, PASS_LAG = 2, 1, 1

learning_rate = 0.1
beta_rate = 0.9
pull_rate = 1.0


def split(value):
    high = value.astype(jnp.bfloat16)
    low = (value - high.astype(jnp.float32)).astype(jnp.bfloat16)
    return high, low


def train_kernel(
    doc_count,
    owners_all,
    counts_all,
    shortlist_all,
    parents,
    embeddings,
    positives,
    weights,
    trained,
    momentum,
    owners,
    counts,
    shortlist,
    emb,
    pos,
    par,
    pull,
    src,
    row_first,
    row_second,
    cand,
    inward,
    outward,
    arrived,
    ready,
    panel,
    load_sem,
    row_send,
    row_recv,
    in_send,
    out_send,
    line_recv,
    shift_send,
    shift_recv,
    spread_send,
    ring_send,
    ring_recv,
    pass_send,
    pass_recv,
):
    doc = lax.axis_index("doc")
    lab = lax.axis_index("lab")
    z, x = lab // RING, lab % RING
    block = doc * (RING * RING) + lab
    width = embeddings.shape[1]
    lanes = width // TILE
    code_rows = lanes * TILE
    part_rows = src.shape[1] // PARTS
    picks = positives.shape[0]
    labels = weights.shape[0]
    scale = 1.0 / (float(width) ** 0.5)
    row = (row_first, row_second)
    span = doc_count // 2
    place = doc % span

    def at_x(k):
        return (doc, z * RING + (x + k) % RING)

    def at_z(to):
        return (doc, to * RING + x)

    def across(k, crosses):
        to_z = jnp.where(crosses, RING - 1 - z, z)
        return ((doc + k) % doc_count, to_z * RING + x)

    def beside(k):
        return ((doc + k) % doc_count, (z + 1 - 2 * (z % 2)) * RING + x)

    sends_over = [place < s for s in range(STEPS)]
    takes_over = [place + s >= span for s in range(STEPS)]

    low_half = z < RING // 2
    side = jnp.where(low_half, 0, 1)
    far = jnp.where(low_half, z + 1, z - 1)
    near = jnp.where(low_half, z - 1, z + 1)
    has_near = (z % (RING - 1)) != 0

    lane_block = pl.ds(TILE * (block // TILE), TILE)
    loads = [
        pltpu.make_async_copy(embeddings, emb, load_sem.at[0]),
        pltpu.make_async_copy(positives, pos, load_sem.at[1]),
        pltpu.make_async_copy(owners_all, owners, load_sem.at[2]),
        pltpu.make_async_copy(counts_all.at[:, lane_block], counts, load_sem.at[3]),
        pltpu.make_async_copy(shortlist_all.at[:, :, lane_block], shortlist, load_sem.at[4]),
        pltpu.make_async_copy(parents.at[pl.ds(8 * (block // 4), 8)], par, load_sem.at[5]),
        pltpu.make_async_copy(weights, trained, load_sem.at[6]),
    ]
    for load in loads:
        load.start()

    barrier = pltpu.get_barrier_semaphore()
    partners = [at_x(k) for k in range(1, RING)]
    for s in range(1, STEPS):
        partners += [across(-s, sends_over[s]), across(s, takes_over[s])]
    partners.append(at_z(far))
    for partner in partners:
        pl.semaphore_signal(barrier, inc=1, device_id=partner, device_id_type=MESH)

    @pl.when(has_near)
    def _():
        pl.semaphore_signal(barrier, inc=1, device_id=at_z(near), device_id_type=MESH)

    expected = len(partners) + jnp.where(has_near, 1, 0)
    for s in range(1, STEPS):
        gives = jnp.logical_and(sends_over[s], jnp.logical_not(has_near))
        gets = jnp.logical_and(takes_over[s], has_near)
        expected += jnp.where(gives, 1, 0) + jnp.where(gets, 1, 0)

        @pl.when(gives)
        def _():
            pl.semaphore_signal(barrier, inc=1, device_id=beside(-s), device_id_type=MESH)

        @pl.when(gets)
        def _():
            pl.semaphore_signal(barrier, inc=1, device_id=beside(s), device_id_type=MESH)

    loads[0].wait()
    loads[1].wait()
    for t in range(RING):
        for c in range(lanes):
            src[t, pl.ds(c * TILE, TILE), :] = emb[pl.ds(t * TILE, TILE), pl.ds(c * TILE, TILE)]
        code = pos[:, pl.ds(t * TILE, TILE)]
        src[t, pl.ds(code_rows, picks), :] = (code // labels).astype(jnp.float32).astype(jnp.bfloat16)
        src[t, pl.ds(code_rows + picks, picks), :] = (code % labels).astype(jnp.float32).astype(jnp.bfloat16)
    for h in range(PARTS):
        row[h][x] = src[x, pl.ds(h * part_rows, part_rows), :]

    pl.semaphore_wait(barrier, expected)

    def remote(source, target, send, recv, device):
        return pltpu.make_async_remote_copy(
            src_ref=source,
            dst_ref=target,
            send_sem=send,
            recv_sem=recv,
            device_id=device,
            device_id_type=MESH,
        )

    parts = [pl.ds(h * part_rows, part_rows) for h in range(PARTS)]

    def row_copies(h):
        return [
            remote(
                src.at[(x + k) % RING, parts[h]],
                row[h].at[x],
                row_send.at[h, k - 1],
                row_recv.at[h, k - 1],
                at_x(k),
            )
            for k in range(1, RING)
        ]

    def row_start(h):
        for copy in row_copies(h):
            copy.start()

    def row_wait(h):
        for copy in row_copies(h):
            copy.wait_recv()

    def owner_z(s, home):
        return owners[s, home] // RING

    def line_in(h, s):
        return remote(
            inward.at[s, parts[h]],
            arrived.at[side, s, parts[h]],
            in_send.at[h, s],
            line_recv.at[side, h, s],
            at_z(far),
        )

    def line_out(h, s, to):
        return remote(
            outward.at[s, parts[h]],
            arrived.at[1 - side, s, parts[h]],
            out_send.at[h, s],
            line_recv.at[1 - side, h, s],
            at_z(to),
        )

    def goes_in(h, s):
        return jnp.logical_or(jnp.logical_not(sends_over[s]), side == h)

    def goes_out(h, s):
        return jnp.logical_or(jnp.logical_not(sends_over[s]), side != h)

    def over_copies(h, s):
        part = outward.at[s, parts[h]]
        target = panel.at[s, x, parts[h]]
        return (
            remote(part, target, spread_send.at[h, s], shift_recv.at[h, s], beside(-s)),
            remote(part, target, shift_send.at[h, s], shift_recv.at[h, s], across(-s, True)),
        )

    def shift_copy(h, s):
        target = panel.at[s, x, parts[h]]
        return remote(
            ready.at[s, parts[h]], target, shift_send.at[h, s], shift_recv.at[h, s], across(-s, False)
        )

    def flow_start(h):
        for s in range(STEPS):
            cand[s, parts[h], :] = row[h][owners[s, doc] % RING]

            @pl.when(jnp.logical_and(goes_in(h, s), jnp.logical_not(has_near)))
            def _():
                inward[s, parts[h], :] = cand[s, parts[h], :]
                line_in(h, s).start()

    def flow_in(h, s):
        @pl.when(jnp.logical_and(goes_in(h, s), has_near))
        def _():
            line_in(h, s).wait_recv()
            inward[s, parts[h], :] = jnp.where(
                owner_z(s, doc) == z, cand[s, parts[h], :], arrived[side, s, parts[h], :]
            )
            line_in(h, s).start()

    def flow_out(h, s):
        mine = owner_z(s, doc) == z

        @pl.when(goes_out(h, s))
        def _():
            line_out(h, s, far).wait_recv()
            outward[s, parts[h], :] = jnp.where(
                mine, cand[s, parts[h], :], arrived[1 - side, s, parts[h], :]
            )

            @pl.when(has_near)
            def _():
                line_out(h, s, near).start()

        over = jnp.logical_and(sends_over[s], side != h)

        @pl.when(jnp.logical_and(over, jnp.logical_not(has_near)))
        def _():
            for copy in over_copies(h, s):
                copy.start()

        @pl.when(jnp.logical_not(sends_over[s]))
        def _():
            nearer = jnp.where(low_half, owner_z(s, doc) <= z, owner_z(s, doc) >= z)
            merged = jnp.where(nearer, inward[s, parts[h], :], arrived[1 - side, s, parts[h], :])
            if s == 0:
                panel[s, x, parts[h], :] = merged
            else:
                ready[s, parts[h], :] = merged
                shift_copy(h, s).start()

    def spread_copy(h, s):
        part = panel.at[s, x, parts[h]]
        to = z + 1 if h < PARTS // 2 else z - 1
        return remote(part, part, spread_send.at[h, s], shift_recv.at[h, s], at_z(to))

    def spreads(h, s):
        passes = z % 2 == (0 if h < PARTS // 2 else 1)
        return jnp.logical_and(takes_over[s], passes)

    def ring_copies(h, s):
        part = panel.at[s, x, parts[h]]
        return (
            remote(part, part, ring_send.at[0, h, s], ring_recv.at[0, h, s], at_x(1)),
            remote(part, part, ring_send.at[1, h, s], ring_recv.at[1, h, s], at_x(-1)),
        )

    def gather(h, s):
        if s > 0:
            shift_copy(h, s).wait_recv()

            @pl.when(spreads(h, s))
            def _():
                spread_copy(h, s).start()

        for copy in ring_copies(h, s):
            copy.start()

    def pass_copy(h, s):
        forth = 1 if h < PARTS // 2 else -1
        part = panel.at[s, (x + RING - forth) % RING, parts[h]]
        return remote(part, part, pass_send.at[h, s], pass_recv.at[h, s], at_x(forth))

    def ring_pass(h, s):
        for copy in ring_copies(h, s):
            copy.wait_recv()
        pass_copy(h, s).start()

    def tile_rows_of(s, t):
        return jnp.concatenate(
            [panel[s, t, pl.ds(c * TILE, TILE), :] for c in range(lanes)], axis=1
        )

    def update(s):
        for h in range(PARTS):
            pass_copy(h, s).wait_recv()
        high, low = split(trained[...])
        count = counts[s, block % TILE]
        grad = None
        for pair in range(RING // 2):
            tiles = (2 * pair, 2 * pair + 1)
            rows = jnp.concatenate([tile_rows_of(s, t) for t in tiles], axis=0)
            contract = (((1,), (1,)), ((), ()))
            scores = (
                lax.dot_general(high, rows, contract, preferred_element_type=jnp.float32)
                + lax.dot_general(low, rows, contract, preferred_element_type=jnp.float32)
            ) * scale
            keys, lives = [], []
            for t in tiles:
                group = panel[s, t, pl.ds(code_rows, picks), :].astype(jnp.float32)
                label = panel[s, t, pl.ds(code_rows + picks, picks), :].astype(jnp.float32)
                wanted = (s * RING * RING + lab).astype(jnp.float32)
                keys.append(jnp.where(group == wanted, label, -1.0))
                live = jnp.float32(0.0)
                for k in range(RING):
                    met = jnp.logical_and(count > k, shortlist[s, k, block % TILE] == t)
                    live = jnp.where(met, jnp.float32(1.0), live)
                lives.append(jnp.full((1, TILE), live, jnp.float32))
            keys = jnp.concatenate(keys, axis=1)
            lives = jnp.concatenate(lives, axis=1)
            names = lax.broadcasted_iota(jnp.int32, scores.shape, 0).astype(jnp.float32)
            hit = names == keys[0:1, :]
            for p in range(1, picks):
                hit = jnp.logical_or(hit, names == keys[p : p + 1, :])
            resid = (jax.nn.sigmoid(scores) - jnp.where(hit, 1.0, 0.0)) * lives
            rhigh, rlow = split(resid)
            part = jnp.dot(rhigh, rows, preferred_element_type=jnp.float32) + jnp.dot(
                rlow, rows, preferred_element_type=jnp.float32
            )
            grad = part if grad is None else grad + part
        pulled = jnp.dot(pull[...], high, preferred_element_type=jnp.float32) + jnp.dot(
            pull[...], low, preferred_element_type=jnp.float32
        )
        moment = beta_rate * momentum[...] + (grad * scale + pull_rate * pulled)
        momentum[...] = moment
        trained[...] = trained[...] - learning_rate * moment

    row_start(0)

    loads[5].wait()
    ids = lax.broadcasted_iota(jnp.int32, (labels, TILE), 0)
    columns = []
    for c in range(labels // TILE):
        parent = par[pl.ds((block % 4) * (labels // TILE) + c, 1), :]
        own = lax.broadcasted_iota(jnp.int32, (labels, TILE), 1) + c * TILE
        columns.append((ids == own).astype(jnp.float32) - (ids == parent).astype(jnp.float32))
    pull[...] = jnp.transpose(jnp.concatenate(columns, axis=1)).astype(jnp.bfloat16)
    momentum[...] = jnp.zeros_like(momentum)
    for load in (loads[2], loads[3], loads[4], loads[6]):
        load.wait()

    row_wait(0)
    row_start(1)
    flow_start(0)
    order = [(h, s) for h in range(PARTS) for s in range(STEPS)]
    units = len(order)

    def when_near(act, h, s):
        if s == 0:
            act(h, s)
        else:

            @pl.when(jnp.logical_not(takes_over[s]))
            def _():
                act(h, s)

    def when_over(act, h, s):
        @pl.when(takes_over[s])
        def _():
            act(h, s)

    for i in range(units + OUT_LAG + GATHER_LAG + PASS_LAG):
        if i == STEPS - 1:
            row_wait(1)
            flow_start(1)
        if i < units:
            flow_in(*order[i])
        i -= OUT_LAG
        if 0 <= i < units:
            flow_out(*order[i])
        i -= GATHER_LAG
        if 0 <= i < units:
            when_near(gather, *order[i])
        i -= PASS_LAG
        if 0 <= i < units:
            when_near(ring_pass, *order[i])
        if i == STEPS + 1:
            update(0)

    late = [(h, s) for h, s in order if s > 0]
    for i, unit in enumerate(late):
        when_over(gather, *unit)
        if i > 0:
            when_over(ring_pass, *late[i - 1])
    update(1)
    when_over(ring_pass, *late[-1])
    update(2)
    update(3)

    for h in range(PARTS):
        for copy in row_copies(h):
            copy.wait_send()
        for s in range(STEPS):

            @pl.when(goes_in(h, s))
            def _():
                line_in(h, s).wait_send()

            @pl.when(jnp.logical_and(goes_out(h, s), has_near))
            def _():
                line_out(h, s, near).wait_send()

            if s > 0:
                ends = jnp.logical_and(side != h, jnp.logical_not(has_near))

                @pl.when(jnp.logical_or(jnp.logical_not(sends_over[s]), ends))
                def _():
                    shift_copy(h, s).wait_send()

                @pl.when(jnp.logical_or(spreads(h, s), jnp.logical_and(sends_over[s], ends)))
                def _():
                    spread_copy(h, s).wait_send()

            for copy in ring_copies(h, s):
                copy.wait_send()
            pass_copy(h, s).wait_send()


def local(doc_count, embeddings, positives, weights, parents, owners, shortlist, counts):
    rows, width = embeddings.shape
    labels = weights.shape[0]
    picks = positives.shape[1]
    slots = shortlist.shape[2]
    tile = (width + 2 * picks, TILE)
    half = jnp.bfloat16
    dma = pltpu.SemaphoreType.DMA
    out = jax.ShapeDtypeStruct(weights.shape, jnp.float32)
    hbm = pl.BlockSpec(memory_space=pltpu.HBM)
    vmem = pl.BlockSpec(memory_space=pltpu.VMEM)
    return pl.pallas_call(
        functools.partial(train_kernel, doc_count),
        out_shape=(out, out),
        in_specs=[hbm] * 7,
        out_specs=(vmem, vmem),
        scratch_shapes=[
            pltpu.SMEM(owners.shape, jnp.int32),
            pltpu.SMEM((STEPS, TILE), jnp.int32),
            pltpu.SMEM((STEPS, slots, TILE), jnp.int32),
            pltpu.VMEM((rows, width), half),
            pltpu.VMEM((picks, rows), jnp.int32),
            pltpu.VMEM((8, TILE), jnp.int32),
            pltpu.VMEM((labels, labels), half),
            pltpu.VMEM((RING,) + tile, half),
            pltpu.VMEM((RING, tile[0] // PARTS, TILE), half),
            pltpu.VMEM((RING, tile[0] // PARTS, TILE), half),
            pltpu.VMEM((STEPS,) + tile, half),
            pltpu.VMEM((STEPS,) + tile, half),
            pltpu.VMEM((STEPS,) + tile, half),
            pltpu.VMEM((2, STEPS) + tile, half),
            pltpu.VMEM((STEPS,) + tile, half),
            pltpu.VMEM((STEPS, RING) + tile, half),
            dma((7,)),
            dma((PARTS, RING - 1)),
            dma((PARTS, RING - 1)),
            dma((PARTS, STEPS)),
            dma((PARTS, STEPS)),
            dma((2, PARTS, STEPS)),
            dma((PARTS, STEPS)),
            dma((PARTS, STEPS)),
            dma((PARTS, STEPS)),
            dma((2, PARTS, STEPS)),
            dma((2, PARTS, STEPS)),
            dma((PARTS, STEPS)),
            dma((PARTS, STEPS)),
        ],
        compiler_params=pltpu.CompilerParams(
            collective_id=0, has_side_effects=True, vmem_limit_bytes=48 * 1024 * 1024
        ),
    )(
        *(
            pltpu.with_memory_space_constraint(value, pltpu.HBM)
            for value in (
                owners,
                counts,
                jnp.transpose(shortlist, (0, 2, 1)),
                parents.reshape(-1, TILE),
                embeddings,
                positives.T,
                weights,
            )
        )
    )


def solution(mesh):
    return jax.shard_map(
        functools.partial(local, mesh.shape["doc"]),
        mesh=mesh,
        in_specs=(
            P(("doc", "lab"), None),
            P(("doc", "lab"), None),
            P(("doc", "lab"), None),
            P(),
            P(),
            P(),
            P(),
        ),
        out_specs=(P(("doc", "lab"), None), P(("doc", "lab"), None)),
        check_vma=False,
    )
```

```python
import functools

import jax
import jax.numpy as jnp
from jax import lax
from jax.experimental import pallas as pl
from jax.experimental.pallas import tpu as pltpu
from jax.sharding import PartitionSpec as P

MESH = pl.DeviceIdType.MESH

TILE = 128
STEPS = 4
RING = 4
PARTS = 4
OUT_LAG, GATHER_LAG, PASS_LAG, UPDATE_LAG = 3, 2, 1, 2

learning_rate = 0.1
beta_rate = 0.9
pull_rate = 1.0


def split(value):
    high = value.astype(jnp.bfloat16)
    low = (value - high.astype(jnp.float32)).astype(jnp.bfloat16)
    return high, low


def part_bounds(rows):
    return [rows // 16 * i // PARTS * 16 for i in range(PARTS + 1)]


def train_kernel(
    doc_count,
    owners_all,
    counts_all,
    shortlist_all,
    parents,
    embeddings,
    positives,
    weights,
    trained,
    momentum,
    owners,
    counts,
    shortlist,
    emb,
    pos,
    par,
    pull,
    src,
    row_0,
    row_1,
    row_2,
    row_3,
    cand,
    inward,
    outward,
    arrived,
    ready,
    panel,
    load_sem,
    row_send,
    row_recv,
    in_send,
    out_send,
    line_recv,
    shift_send,
    shift_recv,
    ring_send,
    ring_recv,
    pass_send,
    pass_recv,
):
    doc = lax.axis_index("doc")
    lab = lax.axis_index("lab")
    z, x = lab // RING, lab % RING
    block = doc * (RING * RING) + lab
    width = embeddings.shape[1]
    lanes = width // TILE
    code_rows = lanes * TILE
    bounds = part_bounds(src.shape[1])
    parts = [pl.ds(a, b - a) for a, b in zip(bounds, bounds[1:])]
    picks = positives.shape[0]
    labels = weights.shape[0]
    scale = 1.0 / (float(width) ** 0.5)
    row = (row_0, row_1, row_2, row_3)
    span = doc_count // 2
    place = doc % span

    def at_x(k):
        return (doc, z * RING + (x + k) % RING)

    def at_z(to):
        return (doc, to * RING + x)

    def across(k, crosses):
        to_z = jnp.where(crosses, RING - 1 - z, z)
        return ((doc + k) % doc_count, to_z * RING + x)

    sends_over = [place < s for s in range(STEPS)]
    takes_over = [place + s >= span for s in range(STEPS)]

    low_half = z < RING // 2
    side = jnp.where(low_half, 0, 1)
    far = jnp.where(low_half, z + 1, z - 1)
    near = jnp.where(low_half, z - 1, z + 1)
    has_near = (z % (RING - 1)) != 0

    lane_block = pl.ds(TILE * (block // TILE), TILE)
    loads = [
        pltpu.make_async_copy(embeddings, emb, load_sem.at[0]),
        pltpu.make_async_copy(positives, pos, load_sem.at[1]),
        pltpu.make_async_copy(owners_all, owners, load_sem.at[2]),
        pltpu.make_async_copy(counts_all.at[:, lane_block], counts, load_sem.at[3]),
        pltpu.make_async_copy(shortlist_all.at[:, :, lane_block], shortlist, load_sem.at[4]),
        pltpu.make_async_copy(parents.at[pl.ds(8 * (block // 4), 8)], par, load_sem.at[5]),
        pltpu.make_async_copy(weights, trained, load_sem.at[6]),
    ]
    for load in loads:
        load.start()

    barrier = pltpu.get_barrier_semaphore()
    partners = [at_x(k) for k in range(1, RING)]
    for s in range(1, STEPS):
        partners += [across(-s, sends_over[s]), across(s, takes_over[s])]
    partners.append(at_z(far))
    for partner in partners:
        pl.semaphore_signal(barrier, inc=1, device_id=partner, device_id_type=MESH)

    @pl.when(has_near)
    def _():
        pl.semaphore_signal(barrier, inc=1, device_id=at_z(near), device_id_type=MESH)

    loads[0].wait()
    loads[1].wait()
    for t in range(RING):
        for c in range(lanes):
            src[t, pl.ds(c * TILE, TILE), :] = emb[pl.ds(t * TILE, TILE), pl.ds(c * TILE, TILE)]
        code = pos[:, pl.ds(t * TILE, TILE)]
        src[t, pl.ds(code_rows, picks), :] = (code // labels).astype(jnp.float32).astype(jnp.bfloat16)
        src[t, pl.ds(code_rows + picks, picks), :] = (code % labels).astype(jnp.float32).astype(jnp.bfloat16)
    for h in range(PARTS):
        row[h][x] = src[x, parts[h], :]

    pl.semaphore_wait(barrier, len(partners) + jnp.where(has_near, 1, 0))

    def remote(source, target, send, recv, device):
        return pltpu.make_async_remote_copy(
            src_ref=source,
            dst_ref=target,
            send_sem=send,
            recv_sem=recv,
            device_id=device,
            device_id_type=MESH,
        )

    def row_copies(h):
        return [
            remote(
                src.at[(x + k) % RING, parts[h]],
                row[h].at[x],
                row_send.at[h, k - 1],
                row_recv.at[h, k - 1],
                at_x(k),
            )
            for k in range(1, RING)
        ]

    def row_start(h):
        for copy in row_copies(h):
            copy.start()

    def row_wait(h):
        for copy in row_copies(h):
            copy.wait_recv()

    def owner_z(s, home):
        return owners[s, home] // RING

    def line_in(h, s):
        return remote(
            inward.at[s, parts[h]],
            arrived.at[side, s, parts[h]],
            in_send.at[h, s],
            line_recv.at[side, h, s],
            at_z(far),
        )

    def line_out(h, s, to):
        return remote(
            outward.at[s, parts[h]],
            arrived.at[1 - side, s, parts[h]],
            out_send.at[h, s],
            line_recv.at[1 - side, h, s],
            at_z(to),
        )

    def shift_copy(h, s):
        target = panel.at[s, x, parts[h]]
        return remote(
            ready.at[s, parts[h]],
            target,
            shift_send.at[h, s],
            shift_recv.at[h, s],
            across(-s, sends_over[s]),
        )

    def flow_start(h):
        for s in range(STEPS):
            cand[s, parts[h], :] = row[h][owners[s, doc] % RING]

            @pl.when(jnp.logical_not(has_near))
            def _():
                inward[s, parts[h], :] = cand[s, parts[h], :]
                line_in(h, s).start()

    def flow_in(h, s):
        @pl.when(has_near)
        def _():
            line_in(h, s).wait_recv()
            inward[s, parts[h], :] = jnp.where(
                owner_z(s, doc) == z, cand[s, parts[h], :], arrived[side, s, parts[h], :]
            )
            line_in(h, s).start()

    def flow_out(h, s):
        line_out(h, s, far).wait_recv()

        @pl.when(has_near)
        def _():
            outward[s, parts[h], :] = jnp.where(
                owner_z(s, doc) == z, cand[s, parts[h], :], arrived[1 - side, s, parts[h], :]
            )
            line_out(h, s, near).start()

        nearer = jnp.where(low_half, owner_z(s, doc) <= z, owner_z(s, doc) >= z)
        merged = jnp.where(nearer, inward[s, parts[h], :], arrived[1 - side, s, parts[h], :])
        if s == 0:
            panel[s, x, parts[h], :] = merged
        else:
            ready[s, parts[h], :] = merged
            shift_copy(h, s).start()

    def ring_copies(h, s):
        part = panel.at[s, x, parts[h]]
        return (
            remote(part, part, ring_send.at[0, h, s], ring_recv.at[0, h, s], at_x(1)),
            remote(part, part, ring_send.at[1, h, s], ring_recv.at[1, h, s], at_x(-1)),
        )

    def gather(h, s):
        if s > 0:
            shift_copy(h, s).wait_recv()

        for copy in ring_copies(h, s):
            copy.start()

    def pass_copy(h, s):
        forth = 1 if h % 2 == 0 else -1
        part = panel.at[s, (x + RING - forth) % RING, parts[h]]
        return remote(part, part, pass_send.at[h, s], pass_recv.at[h, s], at_x(forth))

    def ring_pass(h, s):
        for copy in ring_copies(h, s):
            copy.wait_recv()
        pass_copy(h, s).start()

    def tile_rows_of(s, t):
        return jnp.concatenate(
            [panel[s, t, pl.ds(c * TILE, TILE), :] for c in range(lanes)], axis=1
        )

    def update(s):
        for h in range(PARTS):
            pass_copy(h, s).wait_recv()
        high, low = split(trained[...])
        count = counts[s, block % TILE]
        grad = None
        for pair in range(RING // 2):
            tiles = (2 * pair, 2 * pair + 1)
            rows = jnp.concatenate([tile_rows_of(s, t) for t in tiles], axis=0)
            contract = (((1,), (1,)), ((), ()))
            scores = (
                lax.dot_general(high, rows, contract, preferred_element_type=jnp.float32)
                + lax.dot_general(low, rows, contract, preferred_element_type=jnp.float32)
            ) * scale
            keys, lives = [], []
            for t in tiles:
                group = panel[s, t, pl.ds(code_rows, picks), :].astype(jnp.float32)
                label = panel[s, t, pl.ds(code_rows + picks, picks), :].astype(jnp.float32)
                wanted = (s * RING * RING + lab).astype(jnp.float32)
                keys.append(jnp.where(group == wanted, label, -1.0))
                live = jnp.float32(0.0)
                for k in range(RING):
                    met = jnp.logical_and(count > k, shortlist[s, k, block % TILE] == t)
                    live = jnp.where(met, jnp.float32(1.0), live)
                lives.append(jnp.full((1, TILE), live, jnp.float32))
            keys = jnp.concatenate(keys, axis=1)
            lives = jnp.concatenate(lives, axis=1)
            names = lax.broadcasted_iota(jnp.int32, scores.shape, 0).astype(jnp.float32)
            hit = names == keys[0:1, :]
            for p in range(1, picks):
                hit = jnp.logical_or(hit, names == keys[p : p + 1, :])
            resid = (jax.nn.sigmoid(scores) - jnp.where(hit, 1.0, 0.0)) * lives
            rhigh, rlow = split(resid)
            part = jnp.dot(rhigh, rows, preferred_element_type=jnp.float32) + jnp.dot(
                rlow, rows, preferred_element_type=jnp.float32
            )
            grad = part if grad is None else grad + part
        pulled = jnp.dot(pull[...], high, preferred_element_type=jnp.float32) + jnp.dot(
            pull[...], low, preferred_element_type=jnp.float32
        )
        moment = beta_rate * momentum[...] + (grad * scale + pull_rate * pulled)
        momentum[...] = moment
        trained[...] = trained[...] - learning_rate * moment

    row_start(0)

    loads[5].wait()
    ids = lax.broadcasted_iota(jnp.int32, (labels, TILE), 0)
    columns = []
    for c in range(labels // TILE):
        parent = par[pl.ds((block % 4) * (labels // TILE) + c, 1), :]
        own = lax.broadcasted_iota(jnp.int32, (labels, TILE), 1) + c * TILE
        columns.append((ids == own).astype(jnp.float32) - (ids == parent).astype(jnp.float32))
    pull[...] = jnp.transpose(jnp.concatenate(columns, axis=1)).astype(jnp.bfloat16)
    momentum[...] = jnp.zeros_like(momentum)
    for load in (loads[2], loads[3], loads[4], loads[6]):
        load.wait()

    row_wait(0)
    row_start(1)
    flow_start(0)
    order = [(h, s) for h in range(PARTS) for s in range(STEPS)]
    units = len(order)
    for i in range(units + OUT_LAG + GATHER_LAG + PASS_LAG + UPDATE_LAG):
        h = (i + 2) // STEPS
        if (i + 2) % STEPS == 0 and h < PARTS:
            row_wait(h)
            if h + 1 < PARTS:
                row_start(h + 1)
            flow_start(h)
        if i < units:
            flow_in(*order[i])
        i -= OUT_LAG
        if 0 <= i < units:
            flow_out(*order[i])
        i -= GATHER_LAG
        if 0 <= i < units:
            gather(*order[i])
        i -= PASS_LAG
        if 0 <= i < units:
            ring_pass(*order[i])
        i -= UPDATE_LAG
        if i >= units - STEPS:
            update(i + STEPS - units)

    for h in range(PARTS):
        for copy in row_copies(h):
            copy.wait_send()
        for s in range(STEPS):

            line_in(h, s).wait_send()

            @pl.when(has_near)
            def _():
                line_out(h, s, near).wait_send()

            if s > 0:
                shift_copy(h, s).wait_send()
            for copy in ring_copies(h, s):
                copy.wait_send()
            pass_copy(h, s).wait_send()


def local(doc_count, embeddings, positives, weights, parents, owners, shortlist, counts):
    rows, width = embeddings.shape
    labels = weights.shape[0]
    picks = positives.shape[1]
    slots = shortlist.shape[2]
    tile = (width + 2 * picks, TILE)
    bounds = part_bounds(tile[0])
    half = jnp.bfloat16
    dma = pltpu.SemaphoreType.DMA
    out = jax.ShapeDtypeStruct(weights.shape, jnp.float32)
    hbm = pl.BlockSpec(memory_space=pltpu.HBM)
    vmem = pl.BlockSpec(memory_space=pltpu.VMEM)
    return pl.pallas_call(
        functools.partial(train_kernel, doc_count),
        out_shape=(out, out),
        in_specs=[hbm] * 7,
        out_specs=(vmem, vmem),
        scratch_shapes=[
            pltpu.SMEM(owners.shape, jnp.int32),
            pltpu.SMEM((STEPS, TILE), jnp.int32),
            pltpu.SMEM((STEPS, slots, TILE), jnp.int32),
            pltpu.VMEM((rows, width), half),
            pltpu.VMEM((picks, rows), jnp.int32),
            pltpu.VMEM((8, TILE), jnp.int32),
            pltpu.VMEM((labels, labels), half),
            pltpu.VMEM((RING,) + tile, half),
            *[pltpu.VMEM((RING, b - a, TILE), half) for a, b in zip(bounds, bounds[1:])],
            pltpu.VMEM((STEPS,) + tile, half),
            pltpu.VMEM((STEPS,) + tile, half),
            pltpu.VMEM((STEPS,) + tile, half),
            pltpu.VMEM((2, STEPS) + tile, half),
            pltpu.VMEM((STEPS,) + tile, half),
            pltpu.VMEM((STEPS, RING) + tile, half),
            dma((7,)),
            dma((PARTS, RING - 1)),
            dma((PARTS, RING - 1)),
            dma((PARTS, STEPS)),
            dma((PARTS, STEPS)),
            dma((2, PARTS, STEPS)),
            dma((PARTS, STEPS)),
            dma((PARTS, STEPS)),
            dma((2, PARTS, STEPS)),
            dma((2, PARTS, STEPS)),
            dma((PARTS, STEPS)),
            dma((PARTS, STEPS)),
        ],
        compiler_params=pltpu.CompilerParams(
            collective_id=0, has_side_effects=True, vmem_limit_bytes=48 * 1024 * 1024
        ),
    )(
        *(
            pltpu.with_memory_space_constraint(value, pltpu.HBM)
            for value in (
                owners,
                counts,
                jnp.transpose(shortlist, (0, 2, 1)),
                parents.reshape(-1, TILE),
                embeddings,
                positives.T,
                weights,
            )
        )
    )


def solution(mesh):
    return jax.shard_map(
        functools.partial(local, mesh.shape["doc"]),
        mesh=mesh,
        in_specs=(
            P(("doc", "lab"), None),
            P(("doc", "lab"), None),
            P(("doc", "lab"), None),
            P(),
            P(),
            P(),
            P(),
        ),
        out_specs=(P(("doc", "lab"), None), P(("doc", "lab"), None)),
        check_vma=False,
    )
```

```python
import functools

import jax
import jax.numpy as jnp
from jax import lax
from jax.experimental import pallas as pl
from jax.experimental.pallas import tpu as pltpu
from jax.sharding import PartitionSpec as P

MESH = pl.DeviceIdType.MESH

TILE = 128
STEPS = 4
RING = 4
SIZES = (6, 8, 12, 12, 12)
PARTS = len(SIZES)
AHEAD = 3
OUT_LAG, GATHER_LAG, PASS_LAG, UPDATE_LAG = 3, 1, 2, 2

learning_rate = 0.1
beta_rate = 0.9
pull_rate = 1.0


def split(value):
    high = value.astype(jnp.bfloat16)
    low = (value - high.astype(jnp.float32)).astype(jnp.bfloat16)
    return high, low


def part_bounds(rows):
    return [rows // sum(SIZES) * sum(SIZES[:i]) for i in range(PARTS + 1)]


def train_kernel(
    doc_count,
    owners_all,
    counts_all,
    shortlist_all,
    parents,
    embeddings,
    positives,
    weights,
    trained,
    momentum,
    owners,
    counts,
    shortlist,
    emb,
    pos,
    par,
    pull,
    high,
    low,
    src,
    row_0,
    row_1,
    row_2,
    row_3,
    row_4,
    cand,
    inward,
    outward,
    arrived,
    ready,
    panel,
    load_sem,
    row_send,
    row_recv,
    in_send,
    out_send,
    line_recv,
    shift_send,
    shift_recv,
    ring_send,
    ring_recv,
    pass_send,
    pass_recv,
):
    doc = lax.axis_index("doc")
    lab = lax.axis_index("lab")
    z, x = lab // RING, lab % RING
    block = doc * (RING * RING) + lab
    width = embeddings.shape[1]
    lanes = width // TILE
    code_rows = lanes * TILE
    bounds = part_bounds(src.shape[1])
    parts = [pl.ds(a, b - a) for a, b in zip(bounds, bounds[1:])]
    picks = positives.shape[0]
    labels = weights.shape[0]
    scale = 1.0 / (float(width) ** 0.5)
    row = (row_0, row_1, row_2, row_3, row_4)
    span = doc_count // 2
    place = doc % span

    def at_x(k):
        return (doc, z * RING + (x + k) % RING)

    def at_z(to):
        return (doc, to * RING + x)

    def across(k, crosses):
        to_z = jnp.where(crosses, RING - 1 - z, z)
        return ((doc + k) % doc_count, to_z * RING + x)

    sends_over = [place < s for s in range(STEPS)]
    takes_over = [place + s >= span for s in range(STEPS)]

    low_half = z < RING // 2
    side = jnp.where(low_half, 0, 1)
    far = jnp.where(low_half, z + 1, z - 1)
    near = jnp.where(low_half, z - 1, z + 1)
    has_near = (z % (RING - 1)) != 0

    lane_block = pl.ds(TILE * (block // TILE), TILE)
    loads = [
        pltpu.make_async_copy(embeddings, emb, load_sem.at[0]),
        pltpu.make_async_copy(positives, pos, load_sem.at[1]),
        pltpu.make_async_copy(owners_all, owners, load_sem.at[2]),
        pltpu.make_async_copy(counts_all.at[:, lane_block], counts, load_sem.at[3]),
        pltpu.make_async_copy(shortlist_all.at[:, :, lane_block], shortlist, load_sem.at[4]),
        pltpu.make_async_copy(parents.at[pl.ds(8 * (block // 4), 8)], par, load_sem.at[5]),
        pltpu.make_async_copy(weights, trained, load_sem.at[6]),
    ]
    for load in loads:
        load.start()

    barrier = pltpu.get_barrier_semaphore()
    partners = [at_x(k) for k in range(1, RING)]
    for s in range(1, STEPS):
        partners += [across(-s, sends_over[s]), across(s, takes_over[s])]
    partners.append(at_z(far))
    for partner in partners:
        pl.semaphore_signal(barrier, inc=1, device_id=partner, device_id_type=MESH)

    @pl.when(has_near)
    def _():
        pl.semaphore_signal(barrier, inc=1, device_id=at_z(near), device_id_type=MESH)

    loads[0].wait()
    loads[1].wait()
    for t in range(RING):
        for c in range(lanes):
            src[t, pl.ds(c * TILE, TILE), :] = emb[pl.ds(t * TILE, TILE), pl.ds(c * TILE, TILE)]
        code = pos[:, pl.ds(t * TILE, TILE)]
        src[t, pl.ds(code_rows, picks), :] = (code // labels).astype(jnp.float32).astype(jnp.bfloat16)
        src[t, pl.ds(code_rows + picks, picks), :] = (code % labels).astype(jnp.float32).astype(jnp.bfloat16)
    for h in range(PARTS):
        row[h][x] = src[x, parts[h], :]

    pl.semaphore_wait(barrier, len(partners) + jnp.where(has_near, 1, 0))

    def remote(source, target, send, recv, device):
        return pltpu.make_async_remote_copy(
            src_ref=source,
            dst_ref=target,
            send_sem=send,
            recv_sem=recv,
            device_id=device,
            device_id_type=MESH,
        )

    def row_copies(h):
        return [
            remote(
                src.at[(x + k) % RING, parts[h]],
                row[h].at[x],
                row_send.at[h, k - 1],
                row_recv.at[h, k - 1],
                at_x(k),
            )
            for k in range(1, RING)
        ]

    def row_start(h):
        for copy in row_copies(h):
            copy.start()

    def row_wait(h):
        for copy in row_copies(h):
            copy.wait_recv()

    def owner_z(s, home):
        return owners[s, home] // RING

    def line_in(h, s):
        return remote(
            inward.at[s, parts[h]],
            arrived.at[side, s, parts[h]],
            in_send.at[h, s],
            line_recv.at[side, h, s],
            at_z(far),
        )

    def line_out(h, s, to):
        return remote(
            outward.at[s, parts[h]],
            arrived.at[1 - side, s, parts[h]],
            out_send.at[h, s],
            line_recv.at[1 - side, h, s],
            at_z(to),
        )

    def shift_copy(h, s):
        target = panel.at[s, x, parts[h]]
        return remote(
            ready.at[s, parts[h]],
            target,
            shift_send.at[h, s],
            shift_recv.at[h, s],
            across(-s, sends_over[s]),
        )

    def flow_start(h):
        for s in range(STEPS):
            cand[s, parts[h], :] = row[h][owners[s, doc] % RING]

            @pl.when(jnp.logical_not(has_near))
            def _():
                inward[s, parts[h], :] = cand[s, parts[h], :]
                line_in(h, s).start()

    def flow_in(h, s):
        @pl.when(has_near)
        def _():
            line_in(h, s).wait_recv()
            inward[s, parts[h], :] = jnp.where(
                owner_z(s, doc) == z, cand[s, parts[h], :], arrived[side, s, parts[h], :]
            )
            line_in(h, s).start()

    def flow_out(h, s):
        line_out(h, s, far).wait_recv()

        @pl.when(has_near)
        def _():
            outward[s, parts[h], :] = jnp.where(
                owner_z(s, doc) == z, cand[s, parts[h], :], arrived[1 - side, s, parts[h], :]
            )
            line_out(h, s, near).start()

        nearer = jnp.where(low_half, owner_z(s, doc) <= z, owner_z(s, doc) >= z)
        merged = jnp.where(nearer, inward[s, parts[h], :], arrived[1 - side, s, parts[h], :])
        if s == 0:
            panel[s, x, parts[h], :] = merged
        else:
            ready[s, parts[h], :] = merged
            shift_copy(h, s).start()

    def ring_copies(h, s):
        part = panel.at[s, x, parts[h]]
        return (
            remote(part, part, ring_send.at[0, h, s], ring_recv.at[0, h, s], at_x(1)),
            remote(part, part, ring_send.at[1, h, s], ring_recv.at[1, h, s], at_x(-1)),
        )

    def gather(h, s):
        if s > 0:
            shift_copy(h, s).wait_recv()

        for copy in ring_copies(h, s):
            copy.start()

    def pass_copy(h, s):
        forth = 1 if h % 2 == 0 else -1
        part = panel.at[s, (x + RING - forth) % RING, parts[h]]
        return remote(part, part, pass_send.at[h, s], pass_recv.at[h, s], at_x(forth))

    def ring_pass(h, s):
        for copy in ring_copies(h, s):
            copy.wait_recv()
        pass_copy(h, s).start()

    def tile_rows_of(s, t):
        return jnp.concatenate(
            [panel[s, t, pl.ds(c * TILE, TILE), :] for c in range(lanes)], axis=1
        )

    def prepare(s):
        whigh, wlow = split(trained[...])
        high[...] = whigh
        low[...] = wlow
        pulled = pull_rate * (
            jnp.dot(pull[...], whigh, preferred_element_type=jnp.float32)
            + jnp.dot(pull[...], wlow, preferred_element_type=jnp.float32)
        )
        momentum[...] = pulled if s == 0 else beta_rate * momentum[...] + pulled

    def update(s):
        for h in range(PARTS):
            pass_copy(h, s).wait_recv()
        count = counts[s, block % TILE]
        grad = None
        for pair in range(RING // 2):
            tiles = (2 * pair, 2 * pair + 1)
            rows = jnp.concatenate([tile_rows_of(s, t) for t in tiles], axis=0)
            contract = (((1,), (1,)), ((), ()))
            scores = (
                lax.dot_general(high[...], rows, contract, preferred_element_type=jnp.float32)
                + lax.dot_general(low[...], rows, contract, preferred_element_type=jnp.float32)
            ) * scale
            keys, lives = [], []
            for t in tiles:
                group = panel[s, t, pl.ds(code_rows, picks), :].astype(jnp.float32)
                label = panel[s, t, pl.ds(code_rows + picks, picks), :].astype(jnp.float32)
                wanted = (s * RING * RING + lab).astype(jnp.float32)
                keys.append(jnp.where(group == wanted, label, -1.0))
                live = jnp.float32(0.0)
                for k in range(RING):
                    met = jnp.logical_and(count > k, shortlist[s, k, block % TILE] == t)
                    live = jnp.where(met, jnp.float32(1.0), live)
                lives.append(jnp.full((1, TILE), live, jnp.float32))
            keys = jnp.concatenate(keys, axis=1)
            lives = jnp.concatenate(lives, axis=1)
            names = lax.broadcasted_iota(jnp.int32, scores.shape, 0).astype(jnp.float32)
            hit = names == keys[0:1, :]
            for p in range(1, picks):
                hit = jnp.logical_or(hit, names == keys[p : p + 1, :])
            resid = (jax.nn.sigmoid(scores) - jnp.where(hit, 1.0, 0.0)) * lives
            rhigh, rlow = split(resid)
            part = jnp.dot(rhigh, rows, preferred_element_type=jnp.float32) + jnp.dot(
                rlow, rows, preferred_element_type=jnp.float32
            )
            grad = part if grad is None else grad + part
        moment = momentum[...] + grad * scale
        momentum[...] = moment
        trained[...] = trained[...] - learning_rate * moment
        if s < STEPS - 1:
            prepare(s + 1)

    for h in range(AHEAD):
        row_start(h)

    loads[5].wait()
    ids = lax.broadcasted_iota(jnp.int32, (labels, TILE), 0)
    columns = []
    for c in range(labels // TILE):
        parent = par[pl.ds((block % 4) * (labels // TILE) + c, 1), :]
        own = lax.broadcasted_iota(jnp.int32, (labels, TILE), 1) + c * TILE
        columns.append((ids == own).astype(jnp.float32) - (ids == parent).astype(jnp.float32))
    pull[...] = jnp.transpose(jnp.concatenate(columns, axis=1)).astype(jnp.bfloat16)
    for load in (loads[2], loads[3], loads[4], loads[6]):
        load.wait()
    prepare(0)

    row_wait(0)
    row_start(AHEAD)
    flow_start(0)
    order = [(h, s) for h in range(PARTS) for s in range(STEPS)]
    units = len(order)
    for i in range(units + OUT_LAG + GATHER_LAG + PASS_LAG + UPDATE_LAG):
        h = (i + 3) // STEPS
        if (i + 3) % STEPS == 0 and 0 < h < PARTS:
            row_wait(h)
            if h + AHEAD < PARTS:
                row_start(h + AHEAD)
            flow_start(h)
        if i < units:
            flow_in(*order[i])
        i -= OUT_LAG
        if 0 <= i < units:
            flow_out(*order[i])
        i -= GATHER_LAG
        if 0 <= i < units:
            gather(*order[i])
        i -= PASS_LAG
        if 0 <= i < units:
            ring_pass(*order[i])
        i -= UPDATE_LAG
        if i >= units - STEPS:
            update(i + STEPS - units)

    for h in range(PARTS):
        for copy in row_copies(h):
            copy.wait_send()
        for s in range(STEPS):

            line_in(h, s).wait_send()

            @pl.when(has_near)
            def _():
                line_out(h, s, near).wait_send()

            if s > 0:
                shift_copy(h, s).wait_send()
            for copy in ring_copies(h, s):
                copy.wait_send()
            pass_copy(h, s).wait_send()


def local(doc_count, embeddings, positives, weights, parents, owners, shortlist, counts):
    rows, width = embeddings.shape
    labels = weights.shape[0]
    picks = positives.shape[1]
    slots = shortlist.shape[2]
    tile = (width + 2 * picks, TILE)
    bounds = part_bounds(tile[0])
    half = jnp.bfloat16
    dma = pltpu.SemaphoreType.DMA
    out = jax.ShapeDtypeStruct(weights.shape, jnp.float32)
    hbm = pl.BlockSpec(memory_space=pltpu.HBM)
    vmem = pl.BlockSpec(memory_space=pltpu.VMEM)
    return pl.pallas_call(
        functools.partial(train_kernel, doc_count),
        out_shape=(out, out),
        in_specs=[hbm] * 7,
        out_specs=(vmem, vmem),
        scratch_shapes=[
            pltpu.SMEM(owners.shape, jnp.int32),
            pltpu.SMEM((STEPS, TILE), jnp.int32),
            pltpu.SMEM((STEPS, slots, TILE), jnp.int32),
            pltpu.VMEM((rows, width), half),
            pltpu.VMEM((picks, rows), jnp.int32),
            pltpu.VMEM((8, TILE), jnp.int32),
            pltpu.VMEM((labels, labels), half),
            pltpu.VMEM(weights.shape, half),
            pltpu.VMEM(weights.shape, half),
            pltpu.VMEM((RING,) + tile, half),
            *[pltpu.VMEM((RING, b - a, TILE), half) for a, b in zip(bounds, bounds[1:])],
            pltpu.VMEM((STEPS,) + tile, half),
            pltpu.VMEM((STEPS,) + tile, half),
            pltpu.VMEM((STEPS,) + tile, half),
            pltpu.VMEM((2, STEPS) + tile, half),
            pltpu.VMEM((STEPS,) + tile, half),
            pltpu.VMEM((STEPS, RING) + tile, half),
            dma((7,)),
            dma((PARTS, RING - 1)),
            dma((PARTS, RING - 1)),
            dma((PARTS, STEPS)),
            dma((PARTS, STEPS)),
            dma((2, PARTS, STEPS)),
            dma((PARTS, STEPS)),
            dma((PARTS, STEPS)),
            dma((2, PARTS, STEPS)),
            dma((2, PARTS, STEPS)),
            dma((PARTS, STEPS)),
            dma((PARTS, STEPS)),
        ],
        compiler_params=pltpu.CompilerParams(
            collective_id=0, has_side_effects=True, vmem_limit_bytes=48 * 1024 * 1024
        ),
    )(
        *(
            pltpu.with_memory_space_constraint(value, pltpu.HBM)
            for value in (
                owners,
                counts,
                jnp.transpose(shortlist, (0, 2, 1)),
                parents.reshape(-1, TILE),
                embeddings,
                positives.T,
                weights,
            )
        )
    )


def solution(mesh):
    return jax.shard_map(
        functools.partial(local, mesh.shape["doc"]),
        mesh=mesh,
        in_specs=(
            P(("doc", "lab"), None),
            P(("doc", "lab"), None),
            P(("doc", "lab"), None),
            P(),
            P(),
            P(),
            P(),
        ),
        out_specs=(P(("doc", "lab"), None), P(("doc", "lab"), None)),
        check_vma=False,
    )
```

```python
import functools

import jax
import jax.numpy as jnp
from jax import lax
from jax.experimental import pallas as pl
from jax.experimental.pallas import tpu as pltpu
from jax.sharding import PartitionSpec as P

MESH = pl.DeviceIdType.MESH

TILE = 128
STEPS = 4
RING = 4
SIZES = (8, 14, 14, 14)
PARTS = len(SIZES)
AHEAD = 3
OUT_LAG, GATHER_LAG, PASS_LAG, UPDATE_LAG = 3, 2, 1, 1

learning_rate = 0.1
beta_rate = 0.9
pull_rate = 1.0


def split(value):
    high = value.astype(jnp.bfloat16)
    low = (value - high.astype(jnp.float32)).astype(jnp.bfloat16)
    return high, low


def part_bounds(rows):
    return [rows // sum(SIZES) * sum(SIZES[:i]) for i in range(PARTS + 1)]


def train_kernel(
    doc_count,
    owners_all,
    counts_all,
    shortlist_all,
    parents,
    embeddings,
    positives,
    weights,
    trained,
    momentum,
    last,
    owners,
    counts,
    shortlist,
    emb,
    pos,
    par,
    pull,
    high,
    low,
    src,
    row_0,
    row_1,
    row_2,
    row_3,
    cand,
    inward,
    outward,
    arrived,
    ready,
    panel,
    load_sem,
    row_send,
    row_recv,
    in_send,
    out_send,
    line_recv,
    shift_send,
    shift_recv,
    ring_send,
    ring_recv,
    pass_send,
    pass_recv,
):
    doc = lax.axis_index("doc")
    lab = lax.axis_index("lab")
    z, x = lab // RING, lab % RING
    block = doc * (RING * RING) + lab
    width = embeddings.shape[1]
    lanes = width // TILE
    code_rows = lanes * TILE
    bounds = part_bounds(src.shape[1])
    parts = [pl.ds(a, b - a) for a, b in zip(bounds, bounds[1:])]
    picks = positives.shape[0]
    labels = weights.shape[0]
    scale = 1.0 / (float(width) ** 0.5)
    row = (row_0, row_1, row_2, row_3)
    span = doc_count // 2
    place = doc % span

    def at_x(k):
        return (doc, z * RING + (x + k) % RING)

    def at_z(to):
        return (doc, to * RING + x)

    def across(k, crosses):
        to_z = jnp.where(crosses, RING - 1 - z, z)
        return ((doc + k) % doc_count, to_z * RING + x)

    sends_over = [place < s for s in range(STEPS)]
    takes_over = [place + s >= span for s in range(STEPS)]

    low_half = z < RING // 2
    side = jnp.where(low_half, 0, 1)
    far = jnp.where(low_half, z + 1, z - 1)
    near = jnp.where(low_half, z - 1, z + 1)
    has_near = (z % (RING - 1)) != 0

    lane_block = pl.ds(TILE * (block // TILE), TILE)
    loads = [
        pltpu.make_async_copy(embeddings, emb, load_sem.at[0]),
        pltpu.make_async_copy(positives, pos, load_sem.at[1]),
        pltpu.make_async_copy(owners_all, owners, load_sem.at[2]),
        pltpu.make_async_copy(counts_all.at[:, lane_block], counts, load_sem.at[3]),
        pltpu.make_async_copy(shortlist_all.at[:, :, lane_block], shortlist, load_sem.at[4]),
        pltpu.make_async_copy(parents.at[pl.ds(8 * (block // 4), 8)], par, load_sem.at[5]),
        pltpu.make_async_copy(weights, trained, load_sem.at[6]),
    ]
    for load in loads:
        load.start()

    barrier = pltpu.get_barrier_semaphore()
    partners = [at_x(k) for k in range(1, RING)]
    for s in range(1, STEPS):
        partners += [across(-s, sends_over[s]), across(s, takes_over[s])]
    partners.append(at_z(far))
    for partner in partners:
        pl.semaphore_signal(barrier, inc=1, device_id=partner, device_id_type=MESH)

    @pl.when(has_near)
    def _():
        pl.semaphore_signal(barrier, inc=1, device_id=at_z(near), device_id_type=MESH)

    loads[0].wait()
    loads[1].wait()
    for t in range(RING):
        for c in range(lanes):
            src[t, pl.ds(c * TILE, TILE), :] = emb[pl.ds(t * TILE, TILE), pl.ds(c * TILE, TILE)]
        code = pos[:, pl.ds(t * TILE, TILE)]
        src[t, pl.ds(code_rows, picks), :] = (code // labels).astype(jnp.float32).astype(jnp.bfloat16)
        src[t, pl.ds(code_rows + picks, picks), :] = (code % labels).astype(jnp.float32).astype(jnp.bfloat16)
    for h in range(PARTS):
        row[h][x] = src[x, parts[h], :]

    pl.semaphore_wait(barrier, len(partners) + jnp.where(has_near, 1, 0))

    def remote(source, target, send, recv, device):
        return pltpu.make_async_remote_copy(
            src_ref=source,
            dst_ref=target,
            send_sem=send,
            recv_sem=recv,
            device_id=device,
            device_id_type=MESH,
        )

    def row_copies(h):
        return [
            remote(
                src.at[(x + k) % RING, parts[h]],
                row[h].at[x],
                row_send.at[h, k - 1],
                row_recv.at[h, k - 1],
                at_x(k),
            )
            for k in (2, 1, 3)
        ]

    def row_start(h):
        for copy in row_copies(h):
            copy.start()

    def row_wait(h):
        for copy in row_copies(h):
            copy.wait_recv()

    def owner_z(s, home):
        return owners[s, home] // RING

    def line_in(h, s):
        return remote(
            inward.at[s, parts[h]],
            arrived.at[side, s, parts[h]],
            in_send.at[h, s],
            line_recv.at[side, h, s],
            at_z(far),
        )

    def line_out(h, s, to):
        return remote(
            outward.at[s, parts[h]],
            arrived.at[1 - side, s, parts[h]],
            out_send.at[h, s],
            line_recv.at[1 - side, h, s],
            at_z(to),
        )

    def shift_copy(h, s):
        target = panel.at[s, x, parts[h]]
        return remote(
            ready.at[s, parts[h]],
            target,
            shift_send.at[h, s],
            shift_recv.at[h, s],
            across(-s, sends_over[s]),
        )

    def flow_start(h):
        for s in range(STEPS):
            cand[s, parts[h], :] = row[h][owners[s, doc] % RING]

            @pl.when(jnp.logical_not(has_near))
            def _():
                inward[s, parts[h], :] = cand[s, parts[h], :]
                line_in(h, s).start()

    def flow_in(h, s):
        @pl.when(has_near)
        def _():
            line_in(h, s).wait_recv()
            inward[s, parts[h], :] = jnp.where(
                owner_z(s, doc) == z, cand[s, parts[h], :], arrived[side, s, parts[h], :]
            )
            line_in(h, s).start()

    def flow_out(h, s):
        line_out(h, s, far).wait_recv()

        @pl.when(has_near)
        def _():
            outward[s, parts[h], :] = jnp.where(
                owner_z(s, doc) == z, cand[s, parts[h], :], arrived[1 - side, s, parts[h], :]
            )
            line_out(h, s, near).start()

        nearer = jnp.where(low_half, owner_z(s, doc) <= z, owner_z(s, doc) >= z)
        merged = jnp.where(nearer, inward[s, parts[h], :], arrived[1 - side, s, parts[h], :])
        if s == 0:
            panel[s, x, parts[h], :] = merged
        else:
            ready[s, parts[h], :] = merged
            shift_copy(h, s).start()

    def ring_copies(h, s):
        part = panel.at[s, x, parts[h]]
        return (
            remote(part, part, ring_send.at[0, h, s], ring_recv.at[0, h, s], at_x(1)),
            remote(part, part, ring_send.at[1, h, s], ring_recv.at[1, h, s], at_x(-1)),
        )

    def gather(h, s):
        if s > 0:
            shift_copy(h, s).wait_recv()

        for copy in ring_copies(h, s):
            copy.start()

    def pass_copy(h, s):
        forth = 1 if h % 2 == 0 else -1
        part = panel.at[s, (x + RING - forth) % RING, parts[h]]
        return remote(part, part, pass_send.at[h, s], pass_recv.at[h, s], at_x(forth))

    def ring_pass(h, s):
        for copy in ring_copies(h, s):
            copy.wait_recv()
        pass_copy(h, s).start()

    def tile_rows_of(s, t):
        return jnp.concatenate(
            [panel[s, t, pl.ds(c * TILE, TILE), :] for c in range(lanes)], axis=1
        )

    def prepare(s):
        whigh, wlow = split(trained[...])
        high[...] = whigh
        low[...] = wlow
        pulled = pull_rate * (
            jnp.dot(pull[...], whigh, preferred_element_type=jnp.float32)
            + jnp.dot(pull[...], wlow, preferred_element_type=jnp.float32)
        )
        momentum[...] = pulled if s == 0 else beta_rate * momentum[...] + pulled

    def update(s):
        for h in range(PARTS):
            pass_copy(h, s).wait_recv()
        count = counts[s, block % TILE]
        grad = None
        for pair in range(RING // 2):
            tiles = (2 * pair, 2 * pair + 1)
            rows = jnp.concatenate([tile_rows_of(s, t) for t in tiles], axis=0)
            contract = (((1,), (1,)), ((), ()))
            scores = (
                lax.dot_general(high[...], rows, contract, preferred_element_type=jnp.float32)
                + lax.dot_general(low[...], rows, contract, preferred_element_type=jnp.float32)
            ) * scale
            keys, lives = [], []
            for t in tiles:
                group = panel[s, t, pl.ds(code_rows, picks), :].astype(jnp.float32)
                label = panel[s, t, pl.ds(code_rows + picks, picks), :].astype(jnp.float32)
                wanted = (s * RING * RING + lab).astype(jnp.float32)
                keys.append(jnp.where(group == wanted, label, -1.0))
                live = jnp.float32(0.0)
                for k in range(RING):
                    met = jnp.logical_and(count > k, shortlist[s, k, block % TILE] == t)
                    live = jnp.where(met, jnp.float32(1.0), live)
                lives.append(jnp.full((1, TILE), live, jnp.float32))
            keys = jnp.concatenate(keys, axis=1)
            lives = jnp.concatenate(lives, axis=1)
            names = lax.broadcasted_iota(jnp.int32, scores.shape, 0).astype(jnp.float32)
            hit = names == keys[0:1, :]
            for p in range(1, picks):
                hit = jnp.logical_or(hit, names == keys[p : p + 1, :])
            resid = (jax.nn.sigmoid(scores) - jnp.where(hit, 1.0, 0.0)) * lives
            rhigh, rlow = split(resid)
            part = jnp.dot(rhigh, rows, preferred_element_type=jnp.float32) + jnp.dot(
                rlow, rows, preferred_element_type=jnp.float32
            )
            grad = part if grad is None else grad + part
        if s == STEPS - 1:
            last[...] = grad * scale
            return
        moment = momentum[...] + grad * scale
        momentum[...] = moment
        trained[...] = trained[...] - learning_rate * moment
        prepare(s + 1)

    for h in range(AHEAD):
        row_start(h)

    loads[5].wait()
    ids = lax.broadcasted_iota(jnp.int32, (labels, TILE), 0)
    columns = []
    for c in range(labels // TILE):
        parent = par[pl.ds((block % 4) * (labels // TILE) + c, 1), :]
        own = lax.broadcasted_iota(jnp.int32, (labels, TILE), 1) + c * TILE
        columns.append((ids == own).astype(jnp.float32) - (ids == parent).astype(jnp.float32))
    pull[...] = jnp.transpose(jnp.concatenate(columns, axis=1)).astype(jnp.bfloat16)
    for load in (loads[2], loads[3], loads[4], loads[6]):
        load.wait()
    prepare(0)

    row_wait(0)
    row_start(AHEAD)
    flow_start(0)
    order = [(h, s) for h in range(PARTS) for s in range(STEPS)]
    units = len(order)
    for i in range(units + OUT_LAG + GATHER_LAG + PASS_LAG + UPDATE_LAG):
        h = (i + 3) // STEPS
        if (i + 3) % STEPS == 0 and 0 < h < PARTS:
            row_wait(h)
            if h + AHEAD < PARTS:
                row_start(h + AHEAD)
            flow_start(h)
        if i < units:
            flow_in(*order[i])
        i -= OUT_LAG
        if 0 <= i < units:
            flow_out(*order[i])
        i -= GATHER_LAG
        if 0 <= i < units:
            gather(*order[i])
        i -= PASS_LAG
        if 0 <= i < units:
            ring_pass(*order[i])
        i -= UPDATE_LAG
        if i >= units - STEPS:
            update(i + STEPS - units)

    for h in range(PARTS):
        for copy in row_copies(h):
            copy.wait_send()
        for s in range(STEPS):

            line_in(h, s).wait_send()

            @pl.when(has_near)
            def _():
                line_out(h, s, near).wait_send()

            if s > 0:
                shift_copy(h, s).wait_send()
            for copy in ring_copies(h, s):
                copy.wait_send()
            pass_copy(h, s).wait_send()


def local(doc_count, embeddings, positives, weights, parents, owners, shortlist, counts):
    rows, width = embeddings.shape
    labels = weights.shape[0]
    picks = positives.shape[1]
    slots = shortlist.shape[2]
    tile = (width + 2 * picks, TILE)
    bounds = part_bounds(tile[0])
    half = jnp.bfloat16
    dma = pltpu.SemaphoreType.DMA
    out = jax.ShapeDtypeStruct(weights.shape, jnp.float32)
    hbm = pl.BlockSpec(memory_space=pltpu.HBM)
    vmem = pl.BlockSpec(memory_space=pltpu.VMEM)
    weight, moment, last = pl.pallas_call(
        functools.partial(train_kernel, doc_count),
        out_shape=(out, out, out),
        in_specs=[hbm] * 7,
        out_specs=(vmem, vmem, vmem),
        scratch_shapes=[
            pltpu.SMEM(owners.shape, jnp.int32),
            pltpu.SMEM((STEPS, TILE), jnp.int32),
            pltpu.SMEM((STEPS, slots, TILE), jnp.int32),
            pltpu.VMEM((rows, width), half),
            pltpu.VMEM((picks, rows), jnp.int32),
            pltpu.VMEM((8, TILE), jnp.int32),
            pltpu.VMEM((labels, labels), half),
            pltpu.VMEM(weights.shape, half),
            pltpu.VMEM(weights.shape, half),
            pltpu.VMEM((RING,) + tile, half),
            *[pltpu.VMEM((RING, b - a, TILE), half) for a, b in zip(bounds, bounds[1:])],
            pltpu.VMEM((STEPS,) + tile, half),
            pltpu.VMEM((STEPS,) + tile, half),
            pltpu.VMEM((STEPS,) + tile, half),
            pltpu.VMEM((2, STEPS) + tile, half),
            pltpu.VMEM((STEPS,) + tile, half),
            pltpu.VMEM((STEPS, RING) + tile, half),
            dma((7,)),
            dma((PARTS, RING - 1)),
            dma((PARTS, RING - 1)),
            dma((PARTS, STEPS)),
            dma((PARTS, STEPS)),
            dma((2, PARTS, STEPS)),
            dma((PARTS, STEPS)),
            dma((PARTS, STEPS)),
            dma((2, PARTS, STEPS)),
            dma((2, PARTS, STEPS)),
            dma((PARTS, STEPS)),
            dma((PARTS, STEPS)),
        ],
        compiler_params=pltpu.CompilerParams(
            collective_id=0, has_side_effects=True, vmem_limit_bytes=48 * 1024 * 1024
        ),
    )(
        *(
            pltpu.with_memory_space_constraint(value, pltpu.HBM)
            for value in (
                owners,
                counts,
                jnp.transpose(shortlist, (0, 2, 1)),
                parents.reshape(-1, TILE),
                embeddings,
                positives.T,
                weights,
            )
        )
    )
    moment = moment + last
    return weight - learning_rate * moment, moment


def solution(mesh):
    return jax.shard_map(
        functools.partial(local, mesh.shape["doc"]),
        mesh=mesh,
        in_specs=(
            P(("doc", "lab"), None),
            P(("doc", "lab"), None),
            P(("doc", "lab"), None),
            P(),
            P(),
            P(),
            P(),
        ),
        out_specs=(P(("doc", "lab"), None), P(("doc", "lab"), None)),
        check_vma=False,
    )
```

```python
import functools

import jax
import jax.numpy as jnp
from jax import lax
from jax.experimental import pallas as pl
from jax.experimental.pallas import tpu as pltpu
from jax.sharding import PartitionSpec as P

MESH = pl.DeviceIdType.MESH

TILE = 128
STEPS = 4
RING = 4
SIZES = (8, 10, 10, 12, 10)
PARTS = len(SIZES)
AHEAD = 5
OUT_LAG, GATHER_LAG, PASS_LAG, UPDATE_LAG = 3, 1, 2, 2

learning_rate = 0.1
beta_rate = 0.9
pull_rate = 1.0


def split(value):
    high = value.astype(jnp.bfloat16)
    low = (value - high.astype(jnp.float32)).astype(jnp.bfloat16)
    return high, low


def part_bounds(rows):
    return [rows // sum(SIZES) * sum(SIZES[:i]) for i in range(PARTS + 1)]


def train_kernel(
    doc_count,
    owners_all,
    counts_all,
    shortlist_all,
    parents,
    embeddings,
    positives,
    weights,
    trained,
    momentum,
    last,
    owners,
    counts,
    shortlist,
    emb,
    pos,
    par,
    pull,
    high,
    low,
    src,
    row_0,
    row_1,
    row_2,
    row_3,
    row_4,
    cand,
    inward,
    outward,
    arrived,
    ready,
    panel,
    load_sem,
    row_send,
    row_recv,
    in_send,
    out_send,
    line_recv,
    shift_send,
    shift_recv,
    ring_send,
    ring_recv,
    pass_send,
    pass_recv,
):
    doc = lax.axis_index("doc")
    lab = lax.axis_index("lab")
    z, x = lab // RING, lab % RING
    block = doc * (RING * RING) + lab
    width = embeddings.shape[1]
    lanes = width // TILE
    code_rows = lanes * TILE
    bounds = part_bounds(src.shape[1])
    parts = [pl.ds(a, b - a) for a, b in zip(bounds, bounds[1:])]
    picks = positives.shape[0]
    labels = weights.shape[0]
    scale = 1.0 / (float(width) ** 0.5)
    row = (row_0, row_1, row_2, row_3, row_4)
    span = doc_count // 2
    place = doc % span

    def at_x(k):
        return (doc, z * RING + (x + k) % RING)

    def at_z(to):
        return (doc, to * RING + x)

    def across(k, crosses):
        to_z = jnp.where(crosses, RING - 1 - z, z)
        return ((doc + k) % doc_count, to_z * RING + x)

    sends_over = [place < s for s in range(STEPS)]
    takes_over = [place + s >= span for s in range(STEPS)]

    low_half = z < RING // 2
    side = jnp.where(low_half, 0, 1)
    far = jnp.where(low_half, z + 1, z - 1)
    near = jnp.where(low_half, z - 1, z + 1)
    has_near = (z % (RING - 1)) != 0

    lane_block = pl.ds(TILE * (block // TILE), TILE)
    loads = [
        pltpu.make_async_copy(embeddings, emb, load_sem.at[0]),
        pltpu.make_async_copy(positives, pos, load_sem.at[1]),
        pltpu.make_async_copy(owners_all, owners, load_sem.at[2]),
        pltpu.make_async_copy(counts_all.at[:, lane_block], counts, load_sem.at[3]),
        pltpu.make_async_copy(shortlist_all.at[:, :, lane_block], shortlist, load_sem.at[4]),
        pltpu.make_async_copy(parents.at[pl.ds(8 * (block // 4), 8)], par, load_sem.at[5]),
        pltpu.make_async_copy(weights, trained, load_sem.at[6]),
    ]
    for load in loads:
        load.start()

    barrier = pltpu.get_barrier_semaphore()
    partners = [at_x(k) for k in range(1, RING)]
    for s in range(1, STEPS):
        partners += [across(-s, sends_over[s]), across(s, takes_over[s])]
    partners.append(at_z(far))
    for partner in partners:
        pl.semaphore_signal(barrier, inc=1, device_id=partner, device_id_type=MESH)

    @pl.when(has_near)
    def _():
        pl.semaphore_signal(barrier, inc=1, device_id=at_z(near), device_id_type=MESH)

    loads[0].wait()
    loads[1].wait()
    for t in range(RING):
        for c in range(lanes):
            src[t, pl.ds(c * TILE, TILE), :] = emb[pl.ds(t * TILE, TILE), pl.ds(c * TILE, TILE)]
        code = pos[:, pl.ds(t * TILE, TILE)]
        src[t, pl.ds(code_rows, picks), :] = (code // labels).astype(jnp.float32).astype(jnp.bfloat16)
        src[t, pl.ds(code_rows + picks, picks), :] = (code % labels).astype(jnp.float32).astype(jnp.bfloat16)
    for h in range(PARTS):
        row[h][x] = src[x, parts[h], :]

    pl.semaphore_wait(barrier, len(partners) + jnp.where(has_near, 1, 0))

    def remote(source, target, send, recv, device):
        return pltpu.make_async_remote_copy(
            src_ref=source,
            dst_ref=target,
            send_sem=send,
            recv_sem=recv,
            device_id=device,
            device_id_type=MESH,
        )

    def row_copies(h):
        return [
            remote(
                src.at[(x + k) % RING, parts[h]],
                row[h].at[x],
                row_send.at[h, k - 1],
                row_recv.at[h, k - 1],
                at_x(k),
            )
            for k in (2, 1, 3)
        ]

    def row_start(h):
        for copy in row_copies(h):
            copy.start()

    def row_wait(h):
        for copy in row_copies(h):
            copy.wait_recv()

    def owner_z(s, home):
        return owners[s, home] // RING

    def line_in(h, s):
        return remote(
            inward.at[s, parts[h]],
            arrived.at[side, s, parts[h]],
            in_send.at[h, s],
            line_recv.at[side, h, s],
            at_z(far),
        )

    def line_out(h, s, to):
        return remote(
            outward.at[s, parts[h]],
            arrived.at[1 - side, s, parts[h]],
            out_send.at[h, s],
            line_recv.at[1 - side, h, s],
            at_z(to),
        )

    def shift_copy(h, s):
        target = panel.at[s, x, parts[h]]
        return remote(
            ready.at[s, parts[h]],
            target,
            shift_send.at[h, s],
            shift_recv.at[h, s],
            across(-s, sends_over[s]),
        )

    def flow_start(h):
        for s in range(STEPS):
            cand[s, parts[h], :] = row[h][owners[s, doc] % RING]

            @pl.when(jnp.logical_not(has_near))
            def _():
                inward[s, parts[h], :] = cand[s, parts[h], :]
                line_in(h, s).start()

    def flow_in(h, s):
        @pl.when(has_near)
        def _():
            line_in(h, s).wait_recv()
            inward[s, parts[h], :] = jnp.where(
                owner_z(s, doc) == z, cand[s, parts[h], :], arrived[side, s, parts[h], :]
            )
            line_in(h, s).start()

    def flow_out(h, s):
        line_out(h, s, far).wait_recv()

        @pl.when(has_near)
        def _():
            outward[s, parts[h], :] = jnp.where(
                owner_z(s, doc) == z, cand[s, parts[h], :], arrived[1 - side, s, parts[h], :]
            )
            line_out(h, s, near).start()

        nearer = jnp.where(low_half, owner_z(s, doc) <= z, owner_z(s, doc) >= z)
        merged = jnp.where(nearer, inward[s, parts[h], :], arrived[1 - side, s, parts[h], :])
        if s == 0:
            panel[s, x, parts[h], :] = merged
        else:
            ready[s, parts[h], :] = merged
            shift_copy(h, s).start()

    def ring_copies(h, s):
        part = panel.at[s, x, parts[h]]
        return (
            remote(part, part, ring_send.at[0, h, s], ring_recv.at[0, h, s], at_x(1)),
            remote(part, part, ring_send.at[1, h, s], ring_recv.at[1, h, s], at_x(-1)),
        )

    def gather(h, s):
        if s > 0:
            shift_copy(h, s).wait_recv()

        for copy in ring_copies(h, s):
            copy.start()

    def pass_copy(h, s):
        forth = 1 if h % 2 == 0 else -1
        part = panel.at[s, (x + RING - forth) % RING, parts[h]]
        return remote(part, part, pass_send.at[h, s], pass_recv.at[h, s], at_x(forth))

    def ring_pass(h, s):
        for copy in ring_copies(h, s):
            copy.wait_recv()
        pass_copy(h, s).start()

    def tile_rows_of(s, t):
        return jnp.concatenate(
            [panel[s, t, pl.ds(c * TILE, TILE), :] for c in range(lanes)], axis=1
        )

    def prepare(s):
        whigh, wlow = split(trained[...])
        high[...] = whigh
        low[...] = wlow
        pulled = pull_rate * (
            jnp.dot(pull[...], whigh, preferred_element_type=jnp.float32)
            + jnp.dot(pull[...], wlow, preferred_element_type=jnp.float32)
        )
        momentum[...] = pulled if s == 0 else beta_rate * momentum[...] + pulled

    def update(s):
        for h in range(PARTS):
            pass_copy(h, s).wait_recv()
        count = counts[s, block % TILE]
        grad = None
        for pair in range(RING // 2):
            tiles = (2 * pair, 2 * pair + 1)
            rows = jnp.concatenate([tile_rows_of(s, t) for t in tiles], axis=0)
            contract = (((1,), (1,)), ((), ()))
            scores = (
                lax.dot_general(high[...], rows, contract, preferred_element_type=jnp.float32)
                + lax.dot_general(low[...], rows, contract, preferred_element_type=jnp.float32)
            ) * scale
            keys, lives = [], []
            for t in tiles:
                group = panel[s, t, pl.ds(code_rows, picks), :].astype(jnp.float32)
                label = panel[s, t, pl.ds(code_rows + picks, picks), :].astype(jnp.float32)
                wanted = (s * RING * RING + lab).astype(jnp.float32)
                keys.append(jnp.where(group == wanted, label, -1.0))
                live = jnp.float32(0.0)
                for k in range(RING):
                    met = jnp.logical_and(count > k, shortlist[s, k, block % TILE] == t)
                    live = jnp.where(met, jnp.float32(1.0), live)
                lives.append(jnp.full((1, TILE), live, jnp.float32))
            keys = jnp.concatenate(keys, axis=1)
            lives = jnp.concatenate(lives, axis=1)
            names = lax.broadcasted_iota(jnp.int32, scores.shape, 0).astype(jnp.float32)
            hit = names == keys[0:1, :]
            for p in range(1, picks):
                hit = jnp.logical_or(hit, names == keys[p : p + 1, :])
            resid = (jax.nn.sigmoid(scores) - jnp.where(hit, 1.0, 0.0)) * lives
            rhigh, rlow = split(resid)
            part = jnp.dot(rhigh, rows, preferred_element_type=jnp.float32) + jnp.dot(
                rlow, rows, preferred_element_type=jnp.float32
            )
            grad = part if grad is None else grad + part
        if s == STEPS - 1:
            last[...] = grad * scale
            return
        moment = momentum[...] + grad * scale
        momentum[...] = moment
        trained[...] = trained[...] - learning_rate * moment
        prepare(s + 1)

    for h in range(AHEAD):
        row_start(h)

    loads[5].wait()
    ids = lax.broadcasted_iota(jnp.int32, (labels, TILE), 0)
    columns = []
    for c in range(labels // TILE):
        parent = par[pl.ds((block % 4) * (labels // TILE) + c, 1), :]
        own = lax.broadcasted_iota(jnp.int32, (labels, TILE), 1) + c * TILE
        columns.append((ids == own).astype(jnp.float32) - (ids == parent).astype(jnp.float32))
    pull[...] = jnp.transpose(jnp.concatenate(columns, axis=1)).astype(jnp.bfloat16)
    for load in (loads[2], loads[3], loads[4], loads[6]):
        load.wait()
    prepare(0)

    row_wait(0)
    if AHEAD < PARTS:
        row_start(AHEAD)
    flow_start(0)
    order = [(h, s) for h in range(PARTS) for s in range(STEPS)]
    units = len(order)
    for i in range(units + OUT_LAG + GATHER_LAG + PASS_LAG + UPDATE_LAG):
        h = (i + 3) // STEPS
        if (i + 3) % STEPS == 0 and 0 < h < PARTS:
            row_wait(h)
            if h + AHEAD < PARTS:
                row_start(h + AHEAD)
            flow_start(h)
        if i < units:
            flow_in(*order[i])
        i -= OUT_LAG
        if 0 <= i < units:
            flow_out(*order[i])
        i -= GATHER_LAG
        if 0 <= i < units:
            gather(*order[i])
        i -= PASS_LAG
        if 0 <= i < units:
            ring_pass(*order[i])
        i -= UPDATE_LAG
        if i >= units - STEPS:
            update(i + STEPS - units)

    for h in range(PARTS):
        for copy in row_copies(h):
            copy.wait_send()
        for s in range(STEPS):

            line_in(h, s).wait_send()

            @pl.when(has_near)
            def _():
                line_out(h, s, near).wait_send()

            if s > 0:
                shift_copy(h, s).wait_send()
            for copy in ring_copies(h, s):
                copy.wait_send()
            pass_copy(h, s).wait_send()


def local(doc_count, embeddings, positives, weights, parents, owners, shortlist, counts):
    rows, width = embeddings.shape
    labels = weights.shape[0]
    picks = positives.shape[1]
    slots = shortlist.shape[2]
    tile = (width + 2 * picks, TILE)
    bounds = part_bounds(tile[0])
    half = jnp.bfloat16
    dma = pltpu.SemaphoreType.DMA
    out = jax.ShapeDtypeStruct(weights.shape, jnp.float32)
    hbm = pl.BlockSpec(memory_space=pltpu.HBM)
    vmem = pl.BlockSpec(memory_space=pltpu.VMEM)
    weight, moment, last = pl.pallas_call(
        functools.partial(train_kernel, doc_count),
        out_shape=(out, out, out),
        in_specs=[hbm] * 7,
        out_specs=(vmem, vmem, vmem),
        scratch_shapes=[
            pltpu.SMEM(owners.shape, jnp.int32),
            pltpu.SMEM((STEPS, TILE), jnp.int32),
            pltpu.SMEM((STEPS, slots, TILE), jnp.int32),
            pltpu.VMEM((rows, width), half),
            pltpu.VMEM((picks, rows), jnp.int32),
            pltpu.VMEM((8, TILE), jnp.int32),
            pltpu.VMEM((labels, labels), half),
            pltpu.VMEM(weights.shape, half),
            pltpu.VMEM(weights.shape, half),
            pltpu.VMEM((RING,) + tile, half),
            *[pltpu.VMEM((RING, b - a, TILE), half) for a, b in zip(bounds, bounds[1:])],
            pltpu.VMEM((STEPS,) + tile, half),
            pltpu.VMEM((STEPS,) + tile, half),
            pltpu.VMEM((STEPS,) + tile, half),
            pltpu.VMEM((2, STEPS) + tile, half),
            pltpu.VMEM((STEPS,) + tile, half),
            pltpu.VMEM((STEPS, RING) + tile, half),
            dma((7,)),
            dma((PARTS, RING - 1)),
            dma((PARTS, RING - 1)),
            dma((PARTS, STEPS)),
            dma((PARTS, STEPS)),
            dma((2, PARTS, STEPS)),
            dma((PARTS, STEPS)),
            dma((PARTS, STEPS)),
            dma((2, PARTS, STEPS)),
            dma((2, PARTS, STEPS)),
            dma((PARTS, STEPS)),
            dma((PARTS, STEPS)),
        ],
        compiler_params=pltpu.CompilerParams(
            collective_id=0, has_side_effects=True, vmem_limit_bytes=48 * 1024 * 1024
        ),
    )(
        *(
            pltpu.with_memory_space_constraint(value, pltpu.HBM)
            for value in (
                owners,
                counts,
                jnp.transpose(shortlist, (0, 2, 1)),
                parents.reshape(-1, TILE),
                embeddings,
                positives.T,
                weights,
            )
        )
    )
    moment = moment + last
    return weight - learning_rate * moment, moment


def solution(mesh):
    return jax.shard_map(
        functools.partial(local, mesh.shape["doc"]),
        mesh=mesh,
        in_specs=(
            P(("doc", "lab"), None),
            P(("doc", "lab"), None),
            P(("doc", "lab"), None),
            P(),
            P(),
            P(),
            P(),
        ),
        out_specs=(P(("doc", "lab"), None), P(("doc", "lab"), None)),
        check_vma=False,
    )
```

```python
import functools

import jax
import jax.numpy as jnp
from jax import lax
from jax.experimental import pallas as pl
from jax.experimental.pallas import tpu as pltpu
from jax.sharding import PartitionSpec as P

MESH = pl.DeviceIdType.MESH

TILE = 128
STEPS = 4
RING = 4
SIZES = (7, 12, 16, 15)
PARTS = len(SIZES)
AHEAD = 4
OUT_LAG, GATHER_LAG, PASS_LAG, UPDATE_LAG = 2, 2, 1, 2

learning_rate = 0.1
beta_rate = 0.9
pull_rate = 1.0


def split(value):
    high = value.astype(jnp.bfloat16)
    low = (value - high.astype(jnp.float32)).astype(jnp.bfloat16)
    return high, low


def part_bounds(rows):
    return [rows // sum(SIZES) * sum(SIZES[:i]) for i in range(PARTS + 1)]


def train_kernel(
    doc_count,
    owners_all,
    counts_all,
    shortlist_all,
    parents,
    embeddings,
    positives,
    weights,
    trained,
    momentum,
    last,
    owners,
    counts,
    shortlist,
    emb,
    pos,
    par,
    pull,
    high,
    low,
    src,
    row_0,
    row_1,
    row_2,
    row_3,
    cand,
    inward,
    outward,
    arrived,
    ready,
    panel,
    load_sem,
    row_send,
    row_recv,
    in_send,
    out_send,
    line_recv,
    shift_send,
    shift_recv,
    ring_send,
    ring_recv,
    pass_send,
    pass_recv,
):
    doc = lax.axis_index("doc")
    lab = lax.axis_index("lab")
    z, x = lab // RING, lab % RING
    block = doc * (RING * RING) + lab
    width = embeddings.shape[1]
    lanes = width // TILE
    code_rows = lanes * TILE
    bounds = part_bounds(src.shape[1])
    parts = [pl.ds(a, b - a) for a, b in zip(bounds, bounds[1:])]
    picks = positives.shape[0]
    labels = weights.shape[0]
    scale = 1.0 / (float(width) ** 0.5)
    row = (row_0, row_1, row_2, row_3)
    span = doc_count // 2
    place = doc % span

    def at_x(k):
        return (doc, z * RING + (x + k) % RING)

    def at_z(to):
        return (doc, to * RING + x)

    def across(k, crosses):
        to_z = jnp.where(crosses, RING - 1 - z, z)
        return ((doc + k) % doc_count, to_z * RING + x)

    sends_over = [place < s for s in range(STEPS)]
    takes_over = [place + s >= span for s in range(STEPS)]

    low_half = z < RING // 2
    side = jnp.where(low_half, 0, 1)
    far = jnp.where(low_half, z + 1, z - 1)
    near = jnp.where(low_half, z - 1, z + 1)
    has_near = (z % (RING - 1)) != 0

    lane_block = pl.ds(TILE * (block // TILE), TILE)
    loads = [
        pltpu.make_async_copy(embeddings, emb, load_sem.at[0]),
        pltpu.make_async_copy(positives, pos, load_sem.at[1]),
        pltpu.make_async_copy(owners_all, owners, load_sem.at[2]),
        pltpu.make_async_copy(counts_all.at[:, lane_block], counts, load_sem.at[3]),
        pltpu.make_async_copy(shortlist_all.at[:, :, lane_block], shortlist, load_sem.at[4]),
        pltpu.make_async_copy(parents.at[pl.ds(8 * (block // 4), 8)], par, load_sem.at[5]),
        pltpu.make_async_copy(weights, trained, load_sem.at[6]),
    ]
    for load in loads:
        load.start()

    barrier = pltpu.get_barrier_semaphore()
    partners = [at_x(k) for k in range(1, RING)]
    for s in range(1, STEPS):
        partners += [across(-s, sends_over[s]), across(s, takes_over[s])]
    partners.append(at_z(far))
    for partner in partners:
        pl.semaphore_signal(barrier, inc=1, device_id=partner, device_id_type=MESH)

    @pl.when(has_near)
    def _():
        pl.semaphore_signal(barrier, inc=1, device_id=at_z(near), device_id_type=MESH)

    loads[0].wait()
    loads[1].wait()
    for t in range(RING):
        for c in range(lanes):
            src[t, pl.ds(c * TILE, TILE), :] = emb[pl.ds(t * TILE, TILE), pl.ds(c * TILE, TILE)]
        code = pos[:, pl.ds(t * TILE, TILE)]
        src[t, pl.ds(code_rows, picks), :] = (code // labels).astype(jnp.float32).astype(jnp.bfloat16)
        src[t, pl.ds(code_rows + picks, picks), :] = (code % labels).astype(jnp.float32).astype(jnp.bfloat16)
    for h in range(PARTS):
        row[h][x] = src[x, parts[h], :]

    pl.semaphore_wait(barrier, len(partners) + jnp.where(has_near, 1, 0))

    def remote(source, target, send, recv, device):
        return pltpu.make_async_remote_copy(
            src_ref=source,
            dst_ref=target,
            send_sem=send,
            recv_sem=recv,
            device_id=device,
            device_id_type=MESH,
        )

    def row_copies(h):
        return [
            remote(
                src.at[(x + k) % RING, parts[h]],
                row[h].at[x],
                row_send.at[h, k - 1],
                row_recv.at[h, k - 1],
                at_x(k),
            )
            for k in (2, 1, 3)
        ]

    def row_start(h):
        for copy in row_copies(h):
            copy.start()

    def row_wait(h):
        for copy in row_copies(h):
            copy.wait_recv()

    def owner_z(s, home):
        return owners[s, home] // RING

    def line_in(h, s):
        return remote(
            inward.at[s, parts[h]],
            arrived.at[side, s, parts[h]],
            in_send.at[h, s],
            line_recv.at[side, h, s],
            at_z(far),
        )

    def line_out(h, s, to):
        return remote(
            outward.at[s, parts[h]],
            arrived.at[1 - side, s, parts[h]],
            out_send.at[h, s],
            line_recv.at[1 - side, h, s],
            at_z(to),
        )

    def shift_copy(h, s):
        target = panel.at[s, x, parts[h]]
        return remote(
            ready.at[s, parts[h]],
            target,
            shift_send.at[h, s],
            shift_recv.at[h, s],
            across(-s, sends_over[s]),
        )

    def flow_start(h):
        for s in range(STEPS):
            cand[s, parts[h], :] = row[h][owners[s, doc] % RING]

            @pl.when(jnp.logical_not(has_near))
            def _():
                inward[s, parts[h], :] = cand[s, parts[h], :]
                line_in(h, s).start()

    def flow_in(h, s):
        @pl.when(has_near)
        def _():
            line_in(h, s).wait_recv()
            inward[s, parts[h], :] = jnp.where(
                owner_z(s, doc) == z, cand[s, parts[h], :], arrived[side, s, parts[h], :]
            )
            line_in(h, s).start()

    def flow_out(h, s):
        line_out(h, s, far).wait_recv()

        @pl.when(has_near)
        def _():
            outward[s, parts[h], :] = jnp.where(
                owner_z(s, doc) == z, cand[s, parts[h], :], arrived[1 - side, s, parts[h], :]
            )
            line_out(h, s, near).start()

        nearer = jnp.where(low_half, owner_z(s, doc) <= z, owner_z(s, doc) >= z)
        merged = jnp.where(nearer, inward[s, parts[h], :], arrived[1 - side, s, parts[h], :])
        if s == 0:
            panel[s, x, parts[h], :] = merged
        else:
            ready[s, parts[h], :] = merged
            shift_copy(h, s).start()

    def ring_copies(h, s):
        part = panel.at[s, x, parts[h]]
        return (
            remote(part, part, ring_send.at[0, h, s], ring_recv.at[0, h, s], at_x(1)),
            remote(part, part, ring_send.at[1, h, s], ring_recv.at[1, h, s], at_x(-1)),
        )

    def gather(h, s):
        if s > 0:
            shift_copy(h, s).wait_recv()

        for copy in ring_copies(h, s):
            copy.start()

    def pass_copy(h, s):
        forth = 1 if h % 2 == 0 else -1
        part = panel.at[s, (x + RING - forth) % RING, parts[h]]
        return remote(part, part, pass_send.at[h, s], pass_recv.at[h, s], at_x(forth))

    def ring_pass(h, s):
        for copy in ring_copies(h, s):
            copy.wait_recv()
        pass_copy(h, s).start()

    def tile_rows_of(s, t):
        return jnp.concatenate(
            [panel[s, t, pl.ds(c * TILE, TILE), :] for c in range(lanes)], axis=1
        )

    def prepare(s):
        whigh, wlow = split(trained[...])
        high[...] = whigh
        low[...] = wlow
        pulled = pull_rate * (
            jnp.dot(pull[...], whigh, preferred_element_type=jnp.float32)
            + jnp.dot(pull[...], wlow, preferred_element_type=jnp.float32)
        )
        momentum[...] = pulled if s == 0 else beta_rate * momentum[...] + pulled

    def update(s):
        for h in range(PARTS):
            pass_copy(h, s).wait_recv()
        count = counts[s, block % TILE]
        grad = None
        for pair in range(RING // 2):
            tiles = (2 * pair, 2 * pair + 1)
            rows = jnp.concatenate([tile_rows_of(s, t) for t in tiles], axis=0)
            contract = (((1,), (1,)), ((), ()))
            scores = (
                lax.dot_general(high[...], rows, contract, preferred_element_type=jnp.float32)
                + lax.dot_general(low[...], rows, contract, preferred_element_type=jnp.float32)
            ) * scale
            keys, lives = [], []
            for t in tiles:
                group = panel[s, t, pl.ds(code_rows, picks), :].astype(jnp.float32)
                label = panel[s, t, pl.ds(code_rows + picks, picks), :].astype(jnp.float32)
                wanted = (s * RING * RING + lab).astype(jnp.float32)
                keys.append(jnp.where(group == wanted, label, -1.0))
                live = jnp.float32(0.0)
                for k in range(RING):
                    met = jnp.logical_and(count > k, shortlist[s, k, block % TILE] == t)
                    live = jnp.where(met, jnp.float32(1.0), live)
                lives.append(jnp.full((1, TILE), live, jnp.float32))
            keys = jnp.concatenate(keys, axis=1)
            lives = jnp.concatenate(lives, axis=1)
            names = lax.broadcasted_iota(jnp.int32, scores.shape, 0).astype(jnp.float32)
            hit = names == keys[0:1, :]
            for p in range(1, picks):
                hit = jnp.logical_or(hit, names == keys[p : p + 1, :])
            resid = (jax.nn.sigmoid(scores) - jnp.where(hit, 1.0, 0.0)) * lives
            rhigh, rlow = split(resid)
            part = jnp.dot(rhigh, rows, preferred_element_type=jnp.float32) + jnp.dot(
                rlow, rows, preferred_element_type=jnp.float32
            )
            grad = part if grad is None else grad + part
        if s == STEPS - 1:
            last[...] = grad * scale
            return
        moment = momentum[...] + grad * scale
        momentum[...] = moment
        trained[...] = trained[...] - learning_rate * moment
        prepare(s + 1)

    for h in range(AHEAD):
        row_start(h)

    loads[5].wait()
    ids = lax.broadcasted_iota(jnp.int32, (labels, TILE), 0)
    columns = []
    for c in range(labels // TILE):
        parent = par[pl.ds((block % 4) * (labels // TILE) + c, 1), :]
        own = lax.broadcasted_iota(jnp.int32, (labels, TILE), 1) + c * TILE
        columns.append((ids == own).astype(jnp.float32) - (ids == parent).astype(jnp.float32))
    pull[...] = jnp.transpose(jnp.concatenate(columns, axis=1)).astype(jnp.bfloat16)
    for load in (loads[2], loads[3], loads[4], loads[6]):
        load.wait()
    prepare(0)

    row_wait(0)
    flow_start(0)
    order = [(h, s) for h in range(PARTS) for s in range(STEPS)]
    units = len(order)
    for i in range(units + OUT_LAG + GATHER_LAG + PASS_LAG + UPDATE_LAG):
        h = i // STEPS + 1
        if i % STEPS == 0 and h < PARTS:
            row_wait(h)
            if h + AHEAD < PARTS:
                row_start(h + AHEAD)
            flow_start(h)
        if i < units:
            flow_in(*order[i])
        i -= OUT_LAG
        if 0 <= i < units:
            flow_out(*order[i])
        i -= GATHER_LAG
        if 0 <= i < units:
            gather(*order[i])
        i -= PASS_LAG
        if 0 <= i < units:
            ring_pass(*order[i])
        i -= UPDATE_LAG
        if i >= units - STEPS:
            update(i + STEPS - units)

    for h in range(PARTS):
        for copy in row_copies(h):
            copy.wait_send()
        for s in range(STEPS):

            line_in(h, s).wait_send()

            @pl.when(has_near)
            def _():
                line_out(h, s, near).wait_send()

            if s > 0:
                shift_copy(h, s).wait_send()
            for copy in ring_copies(h, s):
                copy.wait_send()
            pass_copy(h, s).wait_send()


def local(doc_count, embeddings, positives, weights, parents, owners, shortlist, counts):
    rows, width = embeddings.shape
    labels = weights.shape[0]
    picks = positives.shape[1]
    slots = shortlist.shape[2]
    tile = (width + 2 * picks, TILE)
    bounds = part_bounds(tile[0])
    half = jnp.bfloat16
    dma = pltpu.SemaphoreType.DMA
    out = jax.ShapeDtypeStruct(weights.shape, jnp.float32)
    hbm = pl.BlockSpec(memory_space=pltpu.HBM)
    vmem = pl.BlockSpec(memory_space=pltpu.VMEM)
    weight, moment, last = pl.pallas_call(
        functools.partial(train_kernel, doc_count),
        out_shape=(out, out, out),
        in_specs=[hbm] * 7,
        out_specs=(vmem, vmem, vmem),
        scratch_shapes=[
            pltpu.SMEM(owners.shape, jnp.int32),
            pltpu.SMEM((STEPS, TILE), jnp.int32),
            pltpu.SMEM((STEPS, slots, TILE), jnp.int32),
            pltpu.VMEM((rows, width), half),
            pltpu.VMEM((picks, rows), jnp.int32),
            pltpu.VMEM((8, TILE), jnp.int32),
            pltpu.VMEM((labels, labels), half),
            pltpu.VMEM(weights.shape, half),
            pltpu.VMEM(weights.shape, half),
            pltpu.VMEM((RING,) + tile, half),
            *[pltpu.VMEM((RING, b - a, TILE), half) for a, b in zip(bounds, bounds[1:])],
            pltpu.VMEM((STEPS,) + tile, half),
            pltpu.VMEM((STEPS,) + tile, half),
            pltpu.VMEM((STEPS,) + tile, half),
            pltpu.VMEM((2, STEPS) + tile, half),
            pltpu.VMEM((STEPS,) + tile, half),
            pltpu.VMEM((STEPS, RING) + tile, half),
            dma((7,)),
            dma((PARTS, RING - 1)),
            dma((PARTS, RING - 1)),
            dma((PARTS, STEPS)),
            dma((PARTS, STEPS)),
            dma((2, PARTS, STEPS)),
            dma((PARTS, STEPS)),
            dma((PARTS, STEPS)),
            dma((2, PARTS, STEPS)),
            dma((2, PARTS, STEPS)),
            dma((PARTS, STEPS)),
            dma((PARTS, STEPS)),
        ],
        compiler_params=pltpu.CompilerParams(
            collective_id=0, has_side_effects=True, vmem_limit_bytes=48 * 1024 * 1024
        ),
    )(
        *(
            pltpu.with_memory_space_constraint(value, pltpu.HBM)
            for value in (
                owners,
                counts,
                jnp.transpose(shortlist, (0, 2, 1)),
                parents.reshape(-1, TILE),
                embeddings,
                positives.T,
                weights,
            )
        )
    )
    moment = moment + last
    return weight - learning_rate * moment, moment


def solution(mesh):
    return jax.shard_map(
        functools.partial(local, mesh.shape["doc"]),
        mesh=mesh,
        in_specs=(
            P(("doc", "lab"), None),
            P(("doc", "lab"), None),
            P(("doc", "lab"), None),
            P(),
            P(),
            P(),
            P(),
        ),
        out_specs=(P(("doc", "lab"), None), P(("doc", "lab"), None)),
        check_vma=False,
    )
```
